32 devices in a mesh: experts: 4 (over z), context: 4 (over y, x), dp: 2 (over core).
Axes of the slice: x: 2, y: 2, z: 4, core: 2. Of those that a mesh axis runs over, the one named last changes fastest.
Arguments:
- tokens: bfloat16 [8, 4096, 512], P(('experts', 'dp'), 'context'), may hold values from -6 to 6
- attn_gain: float32 [512], replicated, may hold values from 0.5 to 1.5
- mix_gain: float32 [512], replicated, may hold values from 0.5 to 1.5
- query_key_value_weight: bfloat16 [512, 1536], replicated, may hold values from -0.375 to 0.375
- output_weight: bfloat16 [512, 512], replicated, may hold values from -0.75 to 0.75
- router_weight: bfloat16 [512, 8], replicated, may hold values from -0.1875 to 0.1875
- w_in: bfloat16 [8, 512, 2048], P('experts'), may hold values from -1.5 to 1.5
- w_exp_out: bfloat16 [8, 2048, 512], P('experts'), may hold values from -1 to 1
- out_grad: bfloat16 [8, 4096, 512], P(('experts', 'dp'), 'context'), may hold values from -6 to 6
- group_slot: int32 [8, 4096], P(('experts', 'dp'), 'context'), may hold values from 0 to 1023, as said below
- group_routes: int32 [1024, 4], P(('experts', 'context', 'dp')), may hold values from 0 to 7, all different within a row
- route_order: int32 [1024, 4], P(('experts', 'context', 'dp')), may hold values from 0 to 127, as said below
Outputs:
- layer_out: bfloat16 [8, 4096, 512], P(('experts', 'dp'), 'context')
- token_grad: float32 [8, 4096, 512], P(('experts', 'dp'), 'context')
- attn_gain_grad: float32 [512], replicated
- mix_gain_grad: float32 [512], replicated
- qkv_grad: float32 [512, 1536], replicated
- out_proj_grad: float32 [512, 512], replicated
- route_grad: float32 [512, 8], replicated
- expert_in_grad: float32 [8, 512, 2048], P('experts')
- expert_out_grad: float32 [8, 2048, 512], P('experts')
The draws below stay inside these ranges and needn't reach their ends.
Inputs may be any that keep to these rules, and one draw needn't show every extreme that they name: `group_slot`: in each run of 1024 positions c * 1024 to c * 1024 + 1023 of a sequence, every slot appears exactly once. `group_routes`: each row names 4 different experts; every expert is named by some row. `route_order`: in each aligned block of 32 rows, all 128 entries differ.
All inputs are finite; a program needn't handle non-finite values.
Results may differ from the reference program's by a relative error of at most 0.028.
Values may be sent and summed in bfloat16 or wider, within the bound.
A program may use at most 256 MiB of HBM per device.

```python
import math
from functools import partial
import jax
import jax.numpy as jnp
from jax import lax

D = 512
HEADS = 8
HEAD_DIM = 64
FF = 2048
G = 32
BLK = 1024
EXPERTS = 8
K = 4
LEN = 4096
SEQS = 8
GROUPS_DEV = 32
GROUPS = 1024
CAP = 20
N_EXPERTS = 4
N_CONTEXT = 4
N_DP = 2


def block_orders(base_key, block_total, block_width):
    subkeys = jax.random.split(base_key, block_total)

    def single_order(subkey):
        return jax.random.permutation(subkey, block_width)
    return jax.vmap(single_order)(subkeys).astype(jnp.int32)


def draw_group_slot(key, part):
    orders = block_orders(jax.random.fold_in(key, 11), SEQS * (LEN // BLK), BLK)
    return orders.reshape(SEQS, LEN)


def draw_route_order(key, part):
    orders = block_orders(jax.random.fold_in(key, 23), GROUPS // GROUPS_DEV, GROUPS_DEV * K)
    return orders.reshape(GROUPS, K)


def block_scale(stream_key, extent, shards, smallest, largest):
    loudness, own = 1.0, jax.random.fold_in(stream_key, 6)
    for position, blocks in shards:
        steps = jnp.exp(jax.random.uniform(jax.random.fold_in(own, position), (blocks,), jnp.float32, smallest / len(shards), largest / len(shards)))
        loudness = loudness * jnp.repeat(steps, extent[position] // blocks).reshape([-1 if axis == position else 1 for axis in range(len(extent))])
    return loudness


def distinct(key, rows, count, top, lift):
    ranking = jax.random.permutation(jax.random.fold_in(key, 1), count)
    boost = ranking
    for power in range(3):
        boost = boost * boost // count
    boost = boost * lift // count
    chance = jax.random.randint(jax.random.fold_in(key, 2), (rows, count), 0, 4096) + boost
    sure = jax.random.permutation(jax.random.fold_in(key, 3), rows)[jnp.arange(count) % rows]
    chance = jnp.where(jnp.arange(rows)[:, None] == sure[None, :], 1 << 14, chance)
    merit = chance * count + jnp.arange(count)
    return lax.top_k(merit.astype(jnp.int32), top)[1].astype(jnp.int32)


def gaussian(own_key, dims, deviation, bound, cuts=(), kind=jnp.bfloat16):
    array = deviation * jax.random.normal(own_key, dims, jnp.float32)
    if cuts:
        array = array * block_scale(own_key, dims, cuts, -0.22, 0.18)
    return jnp.clip(array, -bound, bound).astype(kind)


def setup_inputs(seed: int = 0) -> dict:
    splits = jax.random.split(jax.random.key(seed), 13)
    tokens = gaussian(splits[0], (SEQS, LEN, D), 1.0, 6.0, ((0, 8), (1, 4)))
    attn_gain = jnp.clip(1.0 + 0.1 * jax.random.normal(splits[1], (D,), jnp.float32), 0.5, 1.5)
    mix_gain = jnp.clip(1.0 + 0.1 * jax.random.normal(splits[2], (D,), jnp.float32), 0.5, 1.5)
    query_key_value_weight = gaussian(splits[3], (D, 3 * D), (D // 2) ** -0.5, 0.375)
    output_weight = gaussian(splits[4], (D, D), (D // 8) ** -0.5, 0.75)
    router_weight = gaussian(splits[5], (D, EXPERTS), (2 * D) ** -0.5, 0.1875)
    w_in = gaussian(splits[6], (EXPERTS, D, FF), (D // 32) ** -0.5, 1.5, ((0, 4),))
    w_exp_out = gaussian(splits[7], (EXPERTS, FF, D), (FF // 64) ** -0.5, 1.0, ((0, 4),))
    out_grad = gaussian(splits[8], (SEQS, LEN, D), 1.0, 6.0, ((0, 8), (1, 4)))
    group_slot = draw_group_slot(jax.random.fold_in(splits[12], 71), 0)
    group_routes = distinct(splits[10], GROUPS, EXPERTS, K, 8192)
    route_order = draw_route_order(jax.random.fold_in(splits[12], 71), 0)
    return {"tokens": tokens, "attn_gain": attn_gain, "mix_gain": mix_gain, "query_key_value_weight": query_key_value_weight, "output_weight": output_weight, "router_weight": router_weight, "w_in": w_in, "w_exp_out": w_exp_out, "out_grad": out_grad, "group_slot": group_slot, "group_routes": group_routes, "route_order": route_order}


@jax.custom_vjp
def low(v):
    return lax.optimization_barrier(v.astype(jnp.bfloat16)).astype(jnp.float32)

@jax.custom_vjp
def low_back(v):
    return v

def low_keep(v):
    return (low(v), None)

def low_pass(kept, grad):
    return (grad,)

def back_keep(v):
    return (v, None)

def back_low(kept, grad):
    return (low(grad),)
low.defvjp(low_keep, low_pass)
low_back.defvjp(back_keep, back_low)
TOP_PRECISION = lax.Precision.HIGHEST
NORM_EPS = 1e-05
MASKED = -1e+30

def smooth_gate(values):
    return jax.nn.gelu(values, approximate=True)

def norm_rows(values, gain):
    inv_rms = lax.rsqrt(lax.optimization_barrier(jnp.mean(values * values, axis=-1, keepdims=True)) + NORM_EPS)
    return values * inv_rms * gain

def attend_block(query_rows, key_rows, value_rows, first_row):
    scores = jnp.einsum('qhd,khd->hqk', query_rows, key_rows, precision=TOP_PRECISION) * HEAD_DIM ** (-0.5)
    scores = low_back(scores)
    query_pos = first_row + jnp.arange(query_rows.shape[0])
    key_pos = jnp.arange(key_rows.shape[0])
    allowed = key_pos[None, None, :] <= query_pos[None, :, None]
    scores = jnp.where(allowed, scores, MASKED)
    probs_full = jax.nn.softmax(scores, axis=-1)
    probs_low = low(probs_full)
    return jnp.einsum('hqk,khd->qhd', probs_low, value_rows, precision=TOP_PRECISION)

def attend_sequence(qkv_rows):
    queries = qkv_rows[:, :D].reshape(LEN, HEADS, HEAD_DIM)
    key_all = qkv_rows[:, D:2 * D].reshape(LEN, HEADS, HEAD_DIM)
    value_all = qkv_rows[:, 2 * D:].reshape(LEN, HEADS, HEAD_DIM)
    block_rows = math.gcd(LEN, 512)
    pieces = []
    for first_row in range(0, LEN, block_rows):
        last_row = first_row + block_rows
        attend = jax.checkpoint(partial(attend_block, first_row=first_row))
        pieces.append(attend(queries[first_row:last_row], key_all[:last_row], value_all[:last_row]))
    return jnp.concatenate(pieces, axis=0).reshape(LEN, D)

def to_devices(values):
    trailing = values.shape[2:]
    blocks = values.reshape((N_EXPERTS, N_DP, N_CONTEXT, BLK) + trailing)
    order_axes = (0, 2, 1, 3) + tuple(range(4, 4 + len(trailing)))
    return blocks.transpose(order_axes).reshape((N_EXPERTS * N_CONTEXT * N_DP, BLK) + trailing)

def from_devices(values):
    trailing = values.shape[2:]
    blocks = values.reshape((N_EXPERTS, N_CONTEXT, N_DP, BLK) + trailing)
    order_axes = (0, 2, 1, 3) + tuple(range(4, 4 + len(trailing)))
    return blocks.transpose(order_axes).reshape((SEQS, LEN) + trailing)

def invert_slots(slot_row):
    return jnp.zeros((BLK,), jnp.int32).at[slot_row].set(jnp.arange(BLK, dtype=jnp.int32))

def pick_rows(table, row_index):
    return table[row_index]

def place_pairs(route_flat, order_flat):
    same_expert = route_flat[:, None] == route_flat[None, :]
    earlier = order_flat[None, :] < order_flat[:, None]
    ranks = lax.optimization_barrier(jnp.sum((same_expert & earlier).astype(jnp.int32), axis=1))
    return jnp.where(ranks < CAP, route_flat * CAP + ranks, EXPERTS * CAP).astype(jnp.int32)

def fill_buffer(pair_index, mixed_rows):
    buffer = jnp.zeros((EXPERTS * CAP + 1, D), mixed_rows.dtype).at[pair_index].add(mixed_rows)
    return buffer[:EXPERTS * CAP]

def expert_apply(packed):
    expert_rows, weight_in, weight_out = packed
    pre_act = low_back(jnp.dot(expert_rows, weight_in, precision=TOP_PRECISION))
    hidden = low(smooth_gate(pre_act))
    return low(low_back(jnp.dot(hidden, weight_out, precision=TOP_PRECISION)))

def layer_forward(tokens, attn_gain, mix_gain, query_key_value_weight, output_weight, router_weight, w_in, w_exp_out, group_slot, group_routes, route_order):
    activation_rows = low(norm_rows(tokens, attn_gain))
    query_key_value = low(low_back(jnp.einsum('kvo,oy->kvy', activation_rows, query_key_value_weight, precision=TOP_PRECISION)))
    attn = lax.map(attend_sequence, query_key_value)
    attention_reduced = low(low_back(attn))
    projected_rows = low_back(jnp.einsum('kvo,oy->kvy', attention_reduced, output_weight, precision=TOP_PRECISION))
    residual = tokens + projected_rows
    mixing_input = low(norm_rows(residual, mix_gain))
    mixing_logits = low_back(jnp.einsum('kvo,oy->kvy', mixing_input, router_weight, precision=TOP_PRECISION))
    device_count = N_EXPERTS * N_CONTEXT * N_DP
    slot_dev = to_devices(group_slot[:, :, None])[:, :, 0]
    inverse = jax.vmap(invert_slots)(slot_dev)
    grouped_in = jax.vmap(pick_rows)(to_devices(mixing_input), inverse).reshape(device_count, GROUPS_DEV, G, D)
    grouped_logit = jax.vmap(pick_rows)(to_devices(mixing_logits), inverse).reshape(device_count, GROUPS_DEV, G, EXPERTS)
    routes_dev = group_routes.reshape(device_count, GROUPS_DEV, K)
    route_index = jnp.broadcast_to(routes_dev[:, :, None, :], (device_count, GROUPS_DEV, G, K))
    chosen = jnp.take_along_axis(grouped_logit, route_index, axis=3)
    weights = jax.nn.softmax(chosen, axis=2)
    mix_low = low(weights)
    mixed = low(low_back(jnp.einsum('vgtk,vgtd->vgkd', mix_low, grouped_in, precision=TOP_PRECISION)))
    pair_index = jax.vmap(place_pairs)(group_routes.reshape(device_count, GROUPS_DEV * K), route_order.reshape(device_count, GROUPS_DEV * K))
    buffers = jax.vmap(fill_buffer)(pair_index, mixed.reshape(device_count, GROUPS_DEV * K, D))
    expert_rows = buffers.reshape(device_count, EXPERTS, CAP, D).transpose(1, 0, 2, 3).reshape(EXPERTS, device_count * CAP, D)
    expert_res = lax.map(jax.checkpoint(expert_apply), (expert_rows, w_in, w_exp_out))
    returned = expert_res.reshape(EXPERTS, device_count, CAP, D).transpose(1, 0, 2, 3).reshape(device_count, EXPERTS * CAP, D)
    padded = jnp.concatenate([returned, jnp.zeros((device_count, 1, D), returned.dtype)], axis=1)
    outputs = jax.vmap(pick_rows)(padded, pair_index).reshape(device_count, GROUPS_DEV, K, D)
    combined = jnp.einsum('vgtk,vgkd->vgtd', mix_low, outputs, precision=TOP_PRECISION).reshape(device_count, BLK, D)
    moe_dev = jax.vmap(pick_rows)(combined, slot_dev)
    return residual + from_devices(moe_dev)

def reference(tokens, attn_gain, mix_gain, query_key_value_weight, output_weight, router_weight, w_in, w_exp_out, out_grad, group_slot, group_routes, route_order):

    def forward(*params):
        return layer_forward(*params, group_slot, group_routes, route_order)
    params = (tokens.astype(jnp.float32), attn_gain.astype(jnp.float32), mix_gain.astype(jnp.float32), query_key_value_weight.astype(jnp.float32), output_weight.astype(jnp.float32), router_weight.astype(jnp.float32), w_in.astype(jnp.float32), w_exp_out.astype(jnp.float32))
    result, pullback = jax.vjp(forward, *params)
    gradients = pullback(out_grad.astype(jnp.float32))
    return (result.astype(jnp.bfloat16), gradients[0], gradients[1], gradients[2], gradients[3], gradients[4], gradients[5], gradients[6], gradients[7])
```

```python
import functools

import jax
import jax.numpy as jnp
import numpy as np
from jax import lax
from jax.experimental import pallas as pl
from jax.experimental.pallas import tpu as pltpu
from jax.sharding import PartitionSpec as P

HEADS = 8
NORM_EPS = 1e-05
MASKED = -1e30
F32 = jnp.float32
BF = jnp.bfloat16
MESH = pl.DeviceIdType.MESH
VMEM = pl.BlockSpec(memory_space=pltpu.VMEM)
ANY = pl.BlockSpec(memory_space=pl.ANY)
LIMIT = 60 << 20
TILE = 512


def dotf(a, b, dims=((1,), (0,)), **kw):
    return lax.dot_general(a, b, (dims, ((), ())), preferred_element_type=F32, **kw)


def params(**kw):
    return pltpu.CompilerParams(vmem_limit_bytes=LIMIT, **kw)


def sequence_of(c):
    return lax.rem(lax.rem(c, 2) + c // 2, 2)


def chip_of(seq, rank):
    return 2 * rank + lax.rem(seq + rank, 2)


def coords():
    return lax.axis_index("context"), lax.axis_index("dp")


def plane_barrier(c, d):
    barrier = pltpu.get_barrier_semaphore()
    for k in range(1, 8):
        other = lax.rem(2 * c + d + k, 8)
        pl.semaphore_signal(
            barrier,
            inc=1,
            device_id={"context": other // 2, "dp": lax.rem(other, 2)},
            device_id_type=MESH,
        )
    pl.semaphore_wait(barrier, 7)


def remote(src, dst, send_sem, recv_sem, context, dp):
    return pltpu.make_async_remote_copy(
        src_ref=src,
        dst_ref=dst,
        send_sem=send_sem,
        recv_sem=recv_sem,
        device_id={"context": context, "dp": dp},
        device_id_type=MESH,
    )


def gather_kernel(x_ref, g_ref, local, full_s, full_r, s1, s2, hr, fs, fr):
    c, d = coords()
    seq = sequence_of(c)
    half = x_ref.shape[0] // 2
    plane_barrier(c, d)
    native = d == seq
    far = 3 - c
    side = 2 * (c // 2) + 1 - lax.rem(c, 2)
    over = 2 * (1 - c // 2) + lax.rem(c, 2)

    def part(ref, e):
        return ref.at[pl.ds(e * half, half)]

    def send(target, e, sem, slot):
        return remote(part(x_ref, e), part(g_ref.at[c], e), sem.at[e], hr.at[slot], target, e)

    @pl.when(native)
    def _():
        for e in range(2):
            send(far, e, s1, 0).start()
        remote(x_ref, g_ref.at[c], full_s, full_r, c, 1 - d).start()
        pltpu.make_async_copy(x_ref, g_ref.at[c], local).start()

    @pl.when(jnp.logical_not(native))
    def _():
        for e in range(2):
            send(side, e, s1, 1).start()
            send(over, e, s2, 2).start()

    forward = []
    for slot, source in ((1, side), (2, over), (0, far)):
        mine = part(g_ref.at[source], d)
        remote(mine, mine, s1.at[0], hr.at[slot], c, d).wait_recv()
        copy = remote(mine, mine, fs.at[slot], fr.at[slot], c, 1 - d)
        copy.start()
        forward.append(copy)

    @pl.when(native)
    def _():
        for e in range(2):
            send(far, e, s1, 0).wait_send()
        remote(x_ref, g_ref.at[c], full_s, full_r, c, 1 - d).wait_send()
        pltpu.make_async_copy(x_ref, g_ref.at[c], local).wait()

    @pl.when(jnp.logical_not(native))
    def _():
        for e in range(2):
            send(side, e, s1, 1).wait_send()
            send(over, e, s2, 2).wait_send()
        remote(x_ref, g_ref.at[c], full_s, full_r, c, 1 - d).wait_recv()

    for copy in forward:
        copy.wait_send()
    for slot, source in ((1, side), (2, over), (0, far)):
        theirs = part(g_ref.at[source], 1 - d)
        remote(theirs, theirs, fs.at[slot], fr.at[slot], c, 1 - d).wait_recv()


def gather_tokens(x, context):
    return pl.pallas_call(
        gather_kernel,
        out_shape=jax.ShapeDtypeStruct((context,) + x.shape, x.dtype),
        in_specs=[ANY],
        out_specs=ANY,
        scratch_shapes=[
            pltpu.SemaphoreType.DMA,
            pltpu.SemaphoreType.DMA,
            pltpu.SemaphoreType.DMA,
            pltpu.SemaphoreType.DMA((2,)),
            pltpu.SemaphoreType.DMA((2,)),
            pltpu.SemaphoreType.DMA((3,)),
            pltpu.SemaphoreType.DMA((3,)),
            pltpu.SemaphoreType.DMA((3,)),
        ],
        compiler_params=params(collective_id=0, has_side_effects=True),
    )(x)


def home_kernel(x_ref, o_ref, local, send, recv):
    c, e = coords()
    seq = sequence_of(c)
    pair = 2 * (c // 2) + e
    plane_barrier(c, e)
    for k in range(4):
        b = lax.rem(c + 3 - k, 4)
        own = jnp.logical_and(b == c, e == seq)

        @pl.when(own)
        def _():
            pltpu.make_async_copy(x_ref.at[b], o_ref.at[pair], local).start()

        @pl.when(jnp.logical_not(own))
        def _():
            remote(x_ref.at[b], o_ref.at[pair], send.at[b], recv.at[pair], b, seq).start()

    for b in range(4):
        own = jnp.logical_and(b == c, e == seq)

        @pl.when(own)
        def _():
            pltpu.make_async_copy(x_ref.at[b], o_ref.at[pair], local).wait()

        @pl.when(jnp.logical_not(own))
        def _():
            remote(x_ref.at[b], o_ref.at[pair], send.at[b], recv.at[pair], b, seq).wait_send()

    for h in range(4):
        own = jnp.logical_and(h == pair, e == seq)

        @pl.when(jnp.logical_not(own))
        def _():
            remote(x_ref.at[h], o_ref.at[h], send.at[h], recv.at[h], c, e).wait_recv()


def to_home(x, cid):
    return pl.pallas_call(
        home_kernel,
        out_shape=jax.ShapeDtypeStruct(x.shape, x.dtype),
        in_specs=[ANY],
        out_specs=ANY,
        scratch_shapes=[
            pltpu.SemaphoreType.DMA,
            pltpu.SemaphoreType.DMA((4,)),
            pltpu.SemaphoreType.DMA((4,)),
        ],
        compiler_params=params(collective_id=cid, has_side_effects=True),
    )(x)


def heads_kernel(x_ref, o_ref, local, send, recv):
    c, d = coords()
    seq = sequence_of(c)
    plane_barrier(c, d)
    for h in range(4):
        chip = chip_of(d, h // 2)
        e = h % 2
        own = jnp.logical_and(chip == c, e == d)

        @pl.when(own)
        def _():
            pltpu.make_async_copy(x_ref.at[h], o_ref.at[c], local).start()

        @pl.when(jnp.logical_not(own))
        def _():
            remote(x_ref.at[h], o_ref.at[c], send.at[h], recv.at[c], chip, e).start()

    for h in range(4):
        chip = chip_of(d, h // 2)
        e = h % 2
        own = jnp.logical_and(chip == c, e == d)

        @pl.when(own)
        def _():
            pltpu.make_async_copy(x_ref.at[h], o_ref.at[c], local).wait()

        @pl.when(jnp.logical_not(own))
        def _():
            remote(x_ref.at[h], o_ref.at[c], send.at[h], recv.at[c], chip, e).wait_send()

    for b in range(4):
        own = jnp.logical_and(b == c, d == seq)

        @pl.when(jnp.logical_not(own))
        def _():
            remote(x_ref.at[b], o_ref.at[b], send.at[b], recv.at[b], c, d).wait_recv()


def to_heads(x, cid):
    return pl.pallas_call(
        heads_kernel,
        out_shape=jax.ShapeDtypeStruct(x.shape, x.dtype),
        in_specs=[ANY],
        out_specs=ANY,
        scratch_shapes=[
            pltpu.SemaphoreType.DMA,
            pltpu.SemaphoreType.DMA((4,)),
            pltpu.SemaphoreType.DMA((4,)),
        ],
        compiler_params=params(collective_id=cid, has_side_effects=True),
    )(x)


def attention_kernel(x_ref, gain_ref, w_ref, qkv_ref, o_ref, lse_ref, ws, vx, acc):
    length = x_ref.shape[0]
    tq, tk = 1024, 512
    c, e = coords()
    pair = 2 * (c // 2) + e
    lane = lax.broadcasted_iota(jnp.int32, (1, 128), 1)
    low = lane < 64
    width = w_ref.shape[0]
    for i in range(3):
        ws[:, 128 * i : 128 * i + 128] = w_ref[
            :, pl.ds(pl.multiple_of(i * width + pair * 128, 128), 128)
        ]

    @pl.loop(0, length // TILE)
    def _(t):
        rows = pl.ds(pl.multiple_of(t * TILE, TILE), TILE)
        x = x_ref[rows, :].astype(F32)
        inv = lax.rsqrt(jnp.mean(x * x, axis=1, keepdims=True) + NORM_EPS)
        act = (x * inv * gain_ref[...]).astype(BF)
        qkv = dotf(act, ws[...]).astype(BF)
        qkv_ref[rows, 0:128] = qkv[:, 0:128] * jnp.asarray(0.125, BF)
        qkv_ref[rows, 128:384] = qkv[:, 128:384]
        vt = jnp.transpose(qkv[:, 256:384].astype(F32)).astype(BF)
        for h in range(2):
            vx[h, 0:64, rows] = vt[64 * h : 64 * h + 64, :]
            vx[h, 64:80, rows] = jnp.ones((16, TILE), BF)

    def step(i, j, qs, carry, diag):
        krows = pl.ds(pl.multiple_of(j * tk, tk), tk)
        k = qkv_ref[krows, 128:256]
        out = []
        first = 0 if diag is None else diag * tk
        cols = slice(first, tq)
        for h in range(2):
            m = carry[h][:, cols]
            s = dotf(k, qs[h][cols, :], ((1,), (1,)))
            if diag is not None:
                kpos = lax.broadcasted_iota(jnp.int32, s.shape, 0)
                qpos = lax.broadcasted_iota(jnp.int32, s.shape, 1)
                s = jnp.where(kpos <= qpos, s, MASKED)
            mn = jnp.maximum(m, jnp.max(s, axis=0, keepdims=True))
            p = jnp.exp(s - mn).astype(BF)
            al = jnp.exp(m - mn)
            acc[h, :, cols] = acc[h, :, cols] * al + dotf(vx[h, :, krows], p)
            if first:
                mn = jnp.concatenate([carry[h][:, :first], mn], axis=1)
            out.append(mn)
        return tuple(out)

    @pl.loop(0, length // tq)
    def _(i):
        rows = pl.ds(pl.multiple_of(i * tq, tq), tq)
        q = qkv_ref[rows, 0:128]
        z = jnp.zeros_like(q)
        qs = [jnp.where(low, q, z), jnp.where(low, z, q)]
        acc[...] = jnp.zeros_like(acc)
        m0 = jnp.full((1, tq), MASKED, F32)
        carry = lax.fori_loop(0, i * (tq // tk), lambda j, m: step(i, j, qs, m, None), (m0, m0))
        for t in range(tq // tk):
            carry = step(i, i * (tq // tk) + t, qs, carry, t)
        parts = []
        for h in range(2):
            total = acc[h, 64:65, :]
            parts.append(acc[h, 0:64, :] / total)
            lse_ref[h : h + 1, rows] = carry[h] + jnp.log(total)
        o_ref[rows, :] = jnp.transpose(jnp.concatenate(parts, axis=0)).astype(BF)


def attention(x, gain, w):
    length = x.shape[0]
    return pl.pallas_call(
        attention_kernel,
        out_shape=(
            jax.ShapeDtypeStruct((length, 384), BF),
            jax.ShapeDtypeStruct((length, 128), BF),
            jax.ShapeDtypeStruct((2, length), F32),
        ),
        in_specs=[VMEM] * 3,
        out_specs=(VMEM,) * 3,
        scratch_shapes=[
            pltpu.VMEM((w.shape[0], 384), BF),
            pltpu.VMEM((2, 80, length), BF),
            pltpu.VMEM((2, 80, 1024), F32),
        ],
        compiler_params=params(),
        name="attention",
    )(x, gain, w)


def attention_back_kernel(qkv_ref, do_ref, o_ref, lse_ref, d_ref, qh, dh, kh, dq, delta):
    length = qkv_ref.shape[0]
    tq = tk = TILE
    low = lax.broadcasted_iota(jnp.int32, (1, 128), 1) < 64
    low_rows = lax.broadcasted_iota(jnp.int32, (128, 1), 0) < 64
    head_sum = (
        lax.broadcasted_iota(jnp.int32, (8, 128), 1) // 64
        == lax.broadcasted_iota(jnp.int32, (8, 128), 0)
    ).astype(F32)

    @pl.loop(0, length // TILE)
    def _(t):
        rows = pl.ds(pl.multiple_of(t * TILE, TILE), TILE)
        q = qkv_ref[rows, 0:128]
        g = do_ref[rows, :]
        z = jnp.zeros_like(q)
        qh[0, rows, :] = jnp.where(low, q, z)
        qh[1, rows, :] = jnp.where(low, z, q)
        dh[0, rows, :] = jnp.where(low, g, z)
        dh[1, rows, :] = jnp.where(low, z, g)
        kt = jnp.transpose(qkv_ref[rows, 128:256].astype(F32)).astype(BF)
        zt = jnp.zeros_like(kt)
        kh[0, :, rows] = jnp.where(low_rows, kt, zt)
        kh[1, :, rows] = jnp.where(low_rows, zt, kt)
        product = g.astype(F32) * o_ref[rows, :].astype(F32)
        delta[:, rows] = dotf(
            head_sum, product, ((1,), (1,)), precision=lax.Precision.HIGHEST
        )
        dq[:, rows] = jnp.zeros((128, TILE), F32)

    def step(i, j, k, v, masked):
        qrows = pl.ds(pl.multiple_of(i * tq, tq), tq)
        krows = pl.ds(pl.multiple_of(j * tk, tk), tk)
        dk = dv = dqt = 0.0
        for h in range(2):
            s = dotf(k, qh[h, qrows, :], ((1,), (1,)))
            p = jnp.exp(s - lse_ref[h : h + 1, qrows])
            if masked:
                kpos = lax.broadcasted_iota(jnp.int32, (tk, tq), 0)
                qpos = lax.broadcasted_iota(jnp.int32, (tk, tq), 1)
                p = jnp.where(kpos <= qpos, p, 0.0)
            dp = dotf(v, dh[h, qrows, :], ((1,), (1,)))
            ds = (p * (dp - delta[h : h + 1, qrows])).astype(BF)
            dv = dv + dotf(p.astype(BF), dh[h, qrows, :])
            dk = dk + dotf(ds, qh[h, qrows, :])
            dqt = dqt + dotf(kh[h, :, krows], ds)
        dq[:, qrows] = dq[:, qrows] + dqt
        return dk, dv

    @pl.loop(0, length // tk)
    def _(j):
        krows = pl.ds(pl.multiple_of(j * tk, tk), tk)
        k = qkv_ref[krows, 128:256]
        v = qkv_ref[krows, 256:384]
        first = step(j, j, k, v, True)

        def body(i, carry):
            dk, dv = step(i, j, k, v, False)
            return carry[0] + dk, carry[1] + dv

        dk, dv = lax.fori_loop(j + 1, length // tq, body, first)
        d_ref[krows, 128:256] = dk.astype(BF)
        d_ref[krows, 256:384] = dv.astype(BF)

    @pl.loop(0, length // TILE)
    def _(t):
        rows = pl.ds(pl.multiple_of(t * TILE, TILE), TILE)
        d_ref[rows, 0:128] = (jnp.transpose(dq[:, rows]) * 0.125).astype(BF)


def attention_back(qkv, do, o, lse):
    length = qkv.shape[0]
    return pl.pallas_call(
        attention_back_kernel,
        out_shape=jax.ShapeDtypeStruct((length, 384), BF),
        in_specs=[VMEM] * 4,
        out_specs=VMEM,
        scratch_shapes=[
            pltpu.VMEM((2, length, 128), BF),
            pltpu.VMEM((2, length, 128), BF),
            pltpu.VMEM((2, 128, length), BF),
            pltpu.VMEM((128, length), F32),
            pltpu.VMEM((8, length), F32),
        ],
        compiler_params=params(),
        name="attention_back",
    )(qkv, do, o, lse)


def mix_kernel(
    stride, capacity, local, choices,
    x_ref, att_ref, wo_ref, gain_ref, router_ref, slot_ref, pair_ref, gout_ref,
    res_ref, mix_ref, wts_ref, place_ref, send_ref,
    att,
):
    tokens = x_ref.shape[0]
    pairs = pair_ref.shape[1]
    experts = router_ref.shape[1]
    members = tokens * choices // pairs
    for h in range(4):
        att[:, 128 * h : 128 * h + 128] = att_ref[h]

    @pl.loop(0, tokens // 256)
    def _(t):
        rows = pl.ds(pl.multiple_of(t * 256, 256), 256)
        res = x_ref[rows, :].astype(F32) + dotf(att[rows, :], wo_ref[...])
        inv = lax.rsqrt(jnp.mean(res * res, axis=1, keepdims=True) + NORM_EPS)
        res_ref[rows, :] = res
        mix_ref[rows, :] = (res * inv * gain_ref[...]).astype(BF)

    routes = pair_ref[0:1, :]
    order = pair_ref[1:2, :]
    eye = lax.broadcasted_iota(jnp.int32, (pairs, pairs), 0) == lax.broadcasted_iota(
        jnp.int32, (pairs, pairs), 1
    )
    zero = jnp.zeros((pairs, pairs), F32)

    def as_column(row):
        return jnp.sum(jnp.where(eye, row.astype(F32), zero), axis=1, keepdims=True)

    route_col = as_column(routes)
    order_col = as_column(order)
    ahead = jnp.logical_and(route_col == routes.astype(F32), order_col < order.astype(F32))
    rank = jnp.sum(ahead.astype(F32), axis=0, keepdims=True).astype(jnp.int32)
    slots = place_ref.shape[0]
    block = lax.div(routes, local)
    place = block * stride + (routes - block * local) * capacity + rank
    place = jnp.where(rank < capacity, place, slots)
    spread = (lax.broadcasted_iota(jnp.int32, (slots, pairs), 0) == place).astype(BF)
    place_ref[...] = spread

    pick = (lax.broadcasted_iota(jnp.int32, (experts, pairs), 0) == routes).astype(F32)
    columns = dotf(router_ref[...].astype(F32), pick).astype(BF)
    chosen = dotf(columns, mix_ref[...], ((0,), (1,)))
    group = lax.broadcasted_iota(jnp.int32, (pairs, 1), 0) // choices
    member = group == slot_ref[...] // members
    chosen = jnp.where(member, chosen, MASKED)
    peak = jnp.max(chosen, axis=1, keepdims=True)
    weight = jnp.where(member, jnp.exp(chosen - peak), 0.0)
    weight = weight / jnp.sum(weight, axis=1, keepdims=True)
    wts_ref[...] = weight
    low = weight.astype(BF)
    width = mix_ref.shape[1]
    mixed = dotf(low, mix_ref[...]).astype(BF)
    send_ref[:, 0:width] = dotf(spread, mixed).astype(BF)
    dy = dotf(low, gout_ref[...]).astype(BF)
    send_ref[:, width:] = dotf(spread, dy).astype(BF)


def gelu_parts(x):
    scale = np.float32(np.sqrt(2.0 / np.pi))
    square = x * x
    t = jnp.tanh(scale * (x + np.float32(0.044715) * (square * x)))
    half = 0.5 * (1.0 + t)
    slope = half + (0.5 * x) * (1.0 - t * t) * (
        scale * (1.0 + np.float32(3 * 0.044715) * square)
    )
    return x * half, slope


def expert_kernel(steps, recv_ref, pick_ref, win_ref, wout_ref, rows_ref, ret_ref, y, dx):
    e = pl.program_id(0)
    f = pl.program_id(1)
    width = win_ref.shape[1]

    @pl.when(f == 0)
    def _():
        rows_ref[0] = dotf(pick_ref[0], recv_ref[...]).astype(BF)
        y[...] = jnp.zeros_like(y)
        dx[...] = jnp.zeros_like(dx)

    @pl.when(jnp.logical_and(e == 0, f == 0))
    def _():
        ret_ref[...] = jnp.zeros_like(ret_ref)

    x = rows_ref[0, :, 0:width]
    dy = rows_ref[0, :, width:]
    hidden, slope = gelu_parts(dotf(x, win_ref[0]))
    y[...] += dotf(hidden.astype(BF), wout_ref[0])
    d_pre = (dotf(dy, wout_ref[0], ((1,), (1,))) * slope).astype(BF)
    dx[...] += dotf(d_pre, win_ref[0], ((1,), (1,)))

    @pl.when(f == steps - 1)
    def _():
        both = jnp.concatenate([y[...].astype(BF), dx[...].astype(BF)], axis=1)
        ret_ref[...] += dotf(pick_ref[0], both, ((0,), (0,))).astype(BF)


def expert_rows(recv, pick, w_in, w_out):
    local, count, total = pick.shape
    _, width, hidden = w_in.shape
    chunk = 512
    steps = hidden // chunk
    return pl.pallas_call(
        functools.partial(expert_kernel, steps),
        grid=(local, steps),
        out_shape=(
            jax.ShapeDtypeStruct((local, count, 2 * width), BF),
            jax.ShapeDtypeStruct((total, 2 * width), BF),
        ),
        in_specs=[
            pl.BlockSpec((total, 2 * width), lambda e, f: (0, 0)),
            pl.BlockSpec((1, count, total), lambda e, f: (e, 0, 0)),
            pl.BlockSpec((1, width, chunk), lambda e, f: (e, 0, f)),
            pl.BlockSpec((1, chunk, width), lambda e, f: (e, f, 0)),
        ],
        out_specs=(
            pl.BlockSpec((1, count, 2 * width), lambda e, f: (e, 0, 0)),
            pl.BlockSpec((total, 2 * width), lambda e, f: (0, 0)),
        ),
        scratch_shapes=[pltpu.VMEM((count, width), F32), pltpu.VMEM((count, width), F32)],
        compiler_params=params(),
        name="expert_rows",
    )(recv, pick, w_in, w_out)


def expert_grad_kernel(rows_ref, win_ref, wout_ref, gin_ref, gout_ref, x, dy):
    width = win_ref.shape[1]
    copies, _, count, _ = rows_ref.shape

    @pl.when(pl.program_id(1) == 0)
    def _():
        for k in range(copies):
            x[k * count : (k + 1) * count, :] = rows_ref[k, 0, :, 0:width]
            dy[k * count : (k + 1) * count, :] = rows_ref[k, 0, :, width:]

    hidden, slope = gelu_parts(dotf(x[...], win_ref[0]))
    d_pre = (dotf(dy[...], wout_ref[0], ((1,), (1,))) * slope).astype(BF)
    gin_ref[0] = dotf(x[...], d_pre, ((0,), (0,)))
    gout_ref[0] = dotf(hidden.astype(BF), dy[...], ((0,), (0,)))


def expert_grads(rows, w_in, w_out):
    copies, local, count, double = rows.shape
    _, width, hidden = w_in.shape
    chunk = 256
    return pl.pallas_call(
        expert_grad_kernel,
        grid=(local, hidden // chunk),
        out_shape=(
            jax.ShapeDtypeStruct(w_in.shape, F32),
            jax.ShapeDtypeStruct(w_out.shape, F32),
        ),
        in_specs=[
            pl.BlockSpec((copies, 1, count, double), lambda e, f: (0, e, 0, 0)),
            pl.BlockSpec((1, width, chunk), lambda e, f: (e, 0, f)),
            pl.BlockSpec((1, chunk, width), lambda e, f: (e, f, 0)),
        ],
        out_specs=(
            pl.BlockSpec((1, width, chunk), lambda e, f: (e, 0, f)),
            pl.BlockSpec((1, chunk, width), lambda e, f: (e, f, 0)),
        ),
        scratch_shapes=[
            pltpu.VMEM((copies * count, width), BF),
            pltpu.VMEM((copies * count, width), BF),
        ],
        compiler_params=params(),
        cost_estimate=pl.CostEstimate(
            flops=8 * copies * local * count * width * hidden,
            bytes_accessed=12 * local * width * hidden,
            transcendentals=copies * local * count * hidden,
        ),
        name="expert_grads",
    )(rows, w_in, w_out)


def unmix_kernel(
    choices,
    res_ref, mix_ref, wts_ref, place_ref, ret_ref, gout_ref, att_ref, wo_ref, gain_ref, router_ref,
    pair_ref,
    out_ref, dres_ref, datt_ref, gproj_ref, small_ref,
    att, dproj, back,
):
    tokens, width = res_ref.shape
    experts = router_ref.shape[1]
    pairs = pair_ref.shape[1]
    rows_back = dotf(place_ref[...], ret_ref[...], ((0,), (0,))).astype(BF)
    y = rows_back[:, 0:width]
    dm = rows_back[:, width:]
    weight = wts_ref[...]
    low = weight.astype(BF)
    dw = dotf(y, gout_ref[...], ((1,), (1,))) + dotf(dm, mix_ref[...], ((1,), (1,)))
    d_chosen = weight * (dw - jnp.sum(weight * dw, axis=1, keepdims=True))
    pick = (
        lax.broadcasted_iota(jnp.int32, (experts, pairs), 0) == pair_ref[0:1, :]
    ).astype(BF)
    d_logits = dotf(pick, d_chosen.astype(BF)).astype(BF)
    small_ref[0:experts, :] = dotf(d_logits, mix_ref[...])
    small_ref[experts:, :] = jnp.zeros((small_ref.shape[0] - experts, width), F32)
    spare = back.shape[0] - pairs - experts
    back[0:pairs, :] = low
    back[pairs : pairs + experts, :] = d_logits
    if spare:
        back[pairs + experts :, :] = jnp.zeros((spare, tokens), BF)
    router_t = jnp.transpose(
        jnp.concatenate(
            [router_ref[...].astype(F32), jnp.zeros((width, 128 - experts), F32)], axis=1
        )
    ).astype(BF)[0 : back.shape[0] - pairs, :]
    for h in range(4):
        att[:, 128 * h : 128 * h + 128] = att_ref[h]
    rhs = jnp.concatenate([dm, router_t], axis=0)
    gain_grad = jnp.zeros((1, width), F32)
    for t in range(tokens // 256):
        rows = slice(t * 256, t * 256 + 256)
        res = res_ref[rows, :]
        combined = dotf(low[:, rows], y, ((0,), (0,)))
        out_ref[rows, :] = (res + combined).astype(BF)
        d_mix = dotf(back[:, rows], rhs, ((0,), (0,)))
        inv = lax.rsqrt(jnp.mean(res * res, axis=1, keepdims=True) + NORM_EPS)
        normed = res * inv
        scaled = d_mix * gain_ref[...]
        gain_grad = gain_grad + jnp.sum(d_mix * normed, axis=0, keepdims=True)
        inner = jnp.mean(scaled * normed, axis=1, keepdims=True)
        d_res = gout_ref[rows, :].astype(F32) + inv * (scaled - normed * inner)
        dres_ref[rows, :] = d_res
        d_low = d_res.astype(BF)
        dproj[rows, :] = d_low
        d_att = dotf(d_low, wo_ref[...], ((1,), (1,))).astype(BF)
        for h in range(4):
            datt_ref[h, rows, :] = d_att[:, 128 * h : 128 * h + 128]
    small_ref[experts : experts + 1, :] = gain_grad
    gproj_ref[...] = dotf(att[...], dproj[...], ((0,), (0,)))


def input_back_kernel(
    dqkv_ref, x_ref, gain_ref, w_ref, dres_ref, tg_ref, gq_ref, gg_ref, act, dqkv
):
    tokens, width = x_ref.shape
    for h in range(4):
        for i in range(3):
            first = i * width + 128 * h
            dqkv[:, first : first + 128] = dqkv_ref[h, :, 128 * i : 128 * i + 128]
    gain_grad = jnp.zeros((1, width), F32)
    for t in range(tokens // 256):
        rows = slice(t * 256, t * 256 + 256)
        x = x_ref[rows, :].astype(F32)
        inv = lax.rsqrt(jnp.mean(x * x, axis=1, keepdims=True) + NORM_EPS)
        normed = x * inv
        act[rows, :] = (normed * gain_ref[...]).astype(BF)
        d_act = dotf(dqkv[rows, :], w_ref[...], ((1,), (1,)))
        scaled = d_act * gain_ref[...]
        gain_grad = gain_grad + jnp.sum(d_act * normed, axis=0, keepdims=True)
        inner = jnp.mean(scaled * normed, axis=1, keepdims=True)
        tg_ref[rows, :] = dres_ref[rows, :] + inv * (scaled - normed * inner)
    gg_ref[...] = gain_grad
    for i in range(3):
        cols = slice(i * width, i * width + width)
        gq_ref[i] = dotf(act[...], dqkv[:, cols], ((0,), (0,)))


def reduce_kernel(
    planes, experts,
    gq_ref, gp_ref, small_ref, extra_ref,
    oq_ref, op_ref, os_ref,
    acc, wire, got0, got1, got2, quarter, gathered, half, slots,
    send0, send1, send2, recv0, recv1, recv2, back0, back1, back2, ssend, srecv,
):
    z = lax.axis_index("experts")
    c, d = coords()
    width = gp_ref.shape[0]
    eighth = got1.shape[1]
    piece = got2.shape[1]
    counts = (2, 4, planes)
    places = (d, c, z)
    axes = ("dp", "context", "experts")
    barrier = pltpu.get_barrier_semaphore()

    def mate(stage, k):
        return {axes[stage]: lax.rem(places[stage] + k, counts[stage])}

    total = 0
    for stage in range(3):
        for k in range(1, counts[stage]):
            pl.semaphore_signal(barrier, inc=1, device_id=mate(stage, k), device_id_type=MESH)
            total += 1
    pl.semaphore_wait(barrier, total)

    def copy(src, dst, send, recv, stage, k):
        return pltpu.make_async_remote_copy(
            src_ref=src, dst_ref=dst, send_sem=send, recv_sem=recv,
            device_id=mate(stage, k), device_id_type=MESH,
        )

    def small_start(stage, value):
        slots[stage, places[stage]] = value
        own = slots.at[stage, places[stage]]
        ops = [
            copy(own, own, ssend.at[stage, k - 1], srecv.at[stage, k - 1], stage, k)
            for k in range(1, counts[stage])
        ]
        for op in ops:
            op.start()
        return ops

    def small_sum(stage, ops):
        for op in ops:
            op.wait()
        value = slots[stage, 0]
        for k in range(1, counts[stage]):
            value = value + slots[stage, k]
        return value

    for i in range(4):
        source = gq_ref.at[i] if i < 3 else gp_ref
        rows = pl.ds((i % 2) * width, width)

        @pl.when(d == i // 2)
        def _():
            acc[rows, :] = source[...]

        @pl.when(d != i // 2)
        def _():
            wire[rows, :] = source[...].astype(BF)

    first = copy(wire, got0, send0, recv0, 0, 1)
    first.start()
    which = lax.broadcasted_iota(jnp.int32, small_ref.shape, 0)
    small = small_ref[...] + jnp.where(which == experts + 1, extra_ref[...], 0.0)
    small_ops = small_start(0, small)
    first.wait()
    acc[...] = acc[...] + got0[...].astype(F32)

    wire[...] = acc[...].astype(BF)
    ops = []
    for k in (2, 1, 3):
        other = lax.rem(c + k, 4)
        op = copy(
            wire.at[pl.ds(other * eighth, eighth)], got1.at[k - 1], send1.at[k - 1], recv1.at[k - 1], 1, k
        )
        op.start()
        ops.append(op)
    small_ops = small_start(1, small_sum(0, small_ops))
    for op in ops:
        op.wait()
    mine = acc[pl.ds(pl.multiple_of(c * eighth, eighth), eighth), :]
    for k in range(3):
        mine = mine + got1[k].astype(F32)
    acc[0:eighth, :] = mine
    quarter[...] = mine.astype(BF)
    ops = []
    for k in range(1, planes):
        other = lax.rem(z + k, planes)
        op = copy(
            quarter.at[pl.ds(other * piece, piece)], got2.at[k - 1], send2.at[k - 1], recv2.at[k - 1], 2, k
        )
        op.start()
        ops.append(op)
    small_ops = small_start(2, small_sum(1, small_ops))
    for op in ops:
        op.wait()
    mine = acc[pl.ds(pl.multiple_of(z * piece, piece), piece), :]
    for k in range(planes - 1):
        mine = mine + got2[k].astype(F32)

    own = pl.ds(pl.multiple_of(z * piece, piece), piece)
    plane_own = pl.ds(pl.multiple_of(c * eighth, eighth), eighth)
    gathered[own, :] = mine.astype(BF)
    ops = []
    for k in range(1, planes):
        op = copy(gathered.at[own], gathered.at[own], send2.at[k - 1], back2.at[k - 1], 2, k)
        op.start()
        ops.append(op)
    os_ref[...] = small_sum(2, small_ops)
    for op in ops:
        op.wait()

    half[d, plane_own, :] = gathered[...]
    ops = []
    for k in (2, 1, 3):
        op = copy(half.at[d, plane_own], half.at[d, plane_own], send1.at[k - 1], back1.at[k - 1], 1, k)
        op.start()
        ops.append(op)
    for op in ops:
        op.wait()

    last = copy(half.at[d], half.at[d], send0, back0, 0, 1)
    last.start()
    last.wait()
    for i in range(4):
        value = half[i // 2, (i % 2) * width : (i % 2 + 1) * width, :].astype(F32)
        if i < 3:
            oq_ref[:, i * width : (i + 1) * width] = value
        else:
            op_ref[...] = value


def reduce_all(gq, gp, small, extra, planes, experts):
    width = gp.shape[0]
    eighth = width // 2
    piece = eighth // planes
    most = max(4, planes)
    dma = pltpu.SemaphoreType.DMA
    return pl.pallas_call(
        functools.partial(reduce_kernel, planes, experts),
        out_shape=(
            jax.ShapeDtypeStruct((width, 3 * width), F32),
            jax.ShapeDtypeStruct((width, width), F32),
            jax.ShapeDtypeStruct(small.shape, F32),
        ),
        in_specs=[VMEM] * 4,
        out_specs=(VMEM,) * 3,
        scratch_shapes=[
            pltpu.VMEM((2 * width, width), F32),
            pltpu.VMEM((2 * width, width), BF),
            pltpu.VMEM((2 * width, width), BF),
            pltpu.VMEM((3, eighth, width), BF),
            pltpu.VMEM((planes - 1, piece, width), BF),
            pltpu.VMEM((eighth, width), BF),
            pltpu.VMEM((eighth, width), BF),
            pltpu.VMEM((2, 2 * width, width), BF),
            pltpu.VMEM((3, most) + small.shape, F32),
            dma, dma((3,)), dma((planes - 1,)),
            dma, dma((3,)), dma((planes - 1,)),
            dma, dma((3,)), dma((planes - 1,)),
            dma((3, most - 1)), dma((3, most - 1)),
        ],
        compiler_params=params(collective_id=5, has_side_effects=True),
        name="reduce_all",
    )(gq, gp, small, extra)


def pick_rows(sources, local, capacity, stride):
    pick = np.zeros((local, sources * capacity, sources * stride), np.float32)
    for e in range(local):
        for r in range(sources * capacity):
            pick[e, r, (r // capacity) * stride + e * capacity + r % capacity] = 1.0
    return pick


def per_device(
    planes,
    tokens,
    attn_gain,
    mix_gain,
    query_key_value_weight,
    output_weight,
    router_weight,
    w_in,
    w_exp_out,
    out_grad,
    group_slot,
    group_routes,
    route_order,
):
    x = tokens[0]
    gout = out_grad[0]
    count, width = x.shape
    groups, choices = group_routes.shape
    pairs = groups * choices
    experts = router_weight.shape[1]
    local = w_in.shape[0]
    sources = experts // local
    capacity = 5 * groups * choices // (4 * experts)
    stride = -(-local * capacity // 16) * 16
    slots = sources * stride
    small_rows = -(-(experts + 2) // 8) * 8
    gain_one = attn_gain.reshape(1, width)
    gain_two = mix_gain.reshape(1, width)
    pair_table = jnp.stack([group_routes.reshape(-1), route_order.reshape(-1)])

    sequence = gather_tokens(x, 4).reshape(4 * count, width)
    qkv, o, lse = attention(sequence, gain_one, query_key_value_weight)
    att = to_home(o.reshape(4, count, 128), 1)

    res, mix, weights, place, send = pl.pallas_call(
        functools.partial(mix_kernel, stride, capacity, local, choices),
        out_shape=(
            jax.ShapeDtypeStruct((count, width), F32),
            jax.ShapeDtypeStruct((count, width), BF),
            jax.ShapeDtypeStruct((pairs, count), F32),
            jax.ShapeDtypeStruct((slots, pairs), BF),
            jax.ShapeDtypeStruct((slots, 2 * width), BF),
        ),
        in_specs=[VMEM] * 8,
        out_specs=(VMEM,) * 5,
        scratch_shapes=[pltpu.VMEM((count, width), BF)],
        compiler_params=params(),
        name="mix",
    )(x, att, output_weight, gain_two, router_weight, group_slot, pair_table, gout)

    recv = lax.all_to_all(
        send.reshape(sources, stride, 2 * width), "experts", split_axis=0, concat_axis=0, tiled=True
    ).reshape(slots, 2 * width)
    pick = jnp.asarray(pick_rows(sources, local, capacity, stride), BF)
    rows, ret = expert_rows(recv, pick, w_in, w_exp_out)
    ret = lax.all_to_all(
        ret.reshape(sources, stride, 2 * width), "experts", split_axis=0, concat_axis=0, tiled=True
    ).reshape(slots, 2 * width)
    all_rows = lax.all_gather(rows, ("context", "dp"), axis=0)

    layer_out, d_res, d_att, g_proj, small = pl.pallas_call(
        functools.partial(unmix_kernel, choices),
        out_shape=(
            jax.ShapeDtypeStruct((count, width), BF),
            jax.ShapeDtypeStruct((count, width), F32),
            jax.ShapeDtypeStruct((4, count, 128), BF),
            jax.ShapeDtypeStruct((width, width), F32),
            jax.ShapeDtypeStruct((small_rows, width), F32),
        ),
        in_specs=[VMEM] * 11,
        out_specs=(VMEM,) * 5,
        scratch_shapes=[
            pltpu.VMEM((count, width), BF),
            pltpu.VMEM((count, width), BF),
            pltpu.VMEM((pairs + -(-experts // 16) * 16, count), BF),
        ],
        compiler_params=params(),
        name="unmix",
    )(
        res, mix, weights, place, ret, gout, att, output_weight, gain_two, router_weight, pair_table
    )

    d_o = to_heads(d_att, 2).reshape(4 * count, 128)
    d_heads = attention_back(qkv, d_o, o, lse)
    d_qkv = to_home(d_heads.reshape(4, count, 384), 3)
    token_grad, g_qkv, g_one = pl.pallas_call(
        input_back_kernel,
        out_shape=(
            jax.ShapeDtypeStruct((count, width), F32),
            jax.ShapeDtypeStruct((3, width, width), F32),
            jax.ShapeDtypeStruct((1, width), F32),
        ),
        in_specs=[VMEM] * 5,
        out_specs=(VMEM,) * 3,
        scratch_shapes=[pltpu.VMEM((count, width), BF), pltpu.VMEM((count, 3 * width), BF)],
        compiler_params=params(),
        name="input_back",
    )(d_qkv, x, gain_one, query_key_value_weight, d_res)
    g_in, g_out = expert_grads(all_rows, w_in, w_exp_out)
    qkv_grad, proj_grad, small = reduce_all(g_qkv, g_proj, small, g_one, planes, experts)
    return (
        layer_out[None],
        token_grad[None],
        small[experts + 1],
        small[experts],
        qkv_grad,
        proj_grad,
        jnp.transpose(small[:experts]),
        g_in,
        g_out,
    )


def solution(mesh):
    token_spec = P(("experts", "dp"), "context", None)
    pair_spec = P(("experts", "context", "dp"), None)
    expert_spec = P("experts", None, None)
    return jax.shard_map(
        functools.partial(per_device, mesh.shape["experts"]),
        mesh=mesh,
        in_specs=(
            token_spec, P(), P(), P(), P(), P(), expert_spec, expert_spec, token_spec,
            P(("experts", "dp"), "context"), pair_spec, pair_spec,
        ),
        out_specs=(
            token_spec, token_spec, P(), P(), P(), P(), P(), expert_spec, expert_spec,
        ),
        check_vma=False,
    )
```

```python
import functools

import jax
import jax.numpy as jnp
import numpy as np
from jax import lax
from jax.experimental import pallas as pl
from jax.experimental.pallas import tpu as pltpu
from jax.sharding import PartitionSpec as P

HEADS = 8
NORM_EPS = 1e-05
MASKED = -1e30
F32 = jnp.float32
BF = jnp.bfloat16
MESH = pl.DeviceIdType.MESH
VMEM = pl.BlockSpec(memory_space=pltpu.VMEM)
ANY = pl.BlockSpec(memory_space=pl.ANY)
LIMIT = 60 << 20
TILE = 512


def dotf(a, b, dims=((1,), (0,)), **kw):
    return lax.dot_general(a, b, (dims, ((), ())), preferred_element_type=F32, **kw)


def params(**kw):
    return pltpu.CompilerParams(vmem_limit_bytes=LIMIT, **kw)


def sequence_of(c):
    return lax.rem(lax.rem(c, 2) + c // 2, 2)


def chip_of(seq, rank):
    return 2 * rank + lax.rem(seq + rank, 2)


def coords():
    return lax.axis_index("context"), lax.axis_index("dp")


def plane_barrier(c, d):
    barrier = pltpu.get_barrier_semaphore()
    for k in range(1, 8):
        other = lax.rem(2 * c + d + k, 8)
        pl.semaphore_signal(
            barrier,
            inc=1,
            device_id={"context": other // 2, "dp": lax.rem(other, 2)},
            device_id_type=MESH,
        )
    pl.semaphore_wait(barrier, 7)


def remote(src, dst, send_sem, recv_sem, context, dp):
    return pltpu.make_async_remote_copy(
        src_ref=src,
        dst_ref=dst,
        send_sem=send_sem,
        recv_sem=recv_sem,
        device_id={"context": context, "dp": dp},
        device_id_type=MESH,
    )


def gather_kernel(x_ref, g_ref, local, full_s, full_r, s1, s2, hr, fs, fr):
    c, d = coords()
    seq = sequence_of(c)
    half = x_ref.shape[0] // 2
    plane_barrier(c, d)
    native = d == seq
    far = 3 - c
    side = 2 * (c // 2) + 1 - lax.rem(c, 2)
    over = 2 * (1 - c // 2) + lax.rem(c, 2)

    def part(ref, e):
        return ref.at[pl.ds(e * half, half)]

    def send(target, e, sem, slot):
        return remote(part(x_ref, e), part(g_ref.at[c], e), sem.at[e], hr.at[slot], target, e)

    @pl.when(native)
    def _():
        for e in range(2):
            send(far, e, s1, 0).start()
        remote(x_ref, g_ref.at[c], full_s, full_r, c, 1 - d).start()
        pltpu.make_async_copy(x_ref, g_ref.at[c], local).start()

    @pl.when(jnp.logical_not(native))
    def _():
        for e in range(2):
            send(side, e, s1, 1).start()
            send(over, e, s2, 2).start()

    forward = []
    for slot, source in ((1, side), (2, over), (0, far)):
        mine = part(g_ref.at[source], d)
        remote(mine, mine, s1.at[0], hr.at[slot], c, d).wait_recv()
        copy = remote(mine, mine, fs.at[slot], fr.at[slot], c, 1 - d)
        copy.start()
        forward.append(copy)

    @pl.when(native)
    def _():
        for e in range(2):
            send(far, e, s1, 0).wait_send()
        remote(x_ref, g_ref.at[c], full_s, full_r, c, 1 - d).wait_send()
        pltpu.make_async_copy(x_ref, g_ref.at[c], local).wait()

    @pl.when(jnp.logical_not(native))
    def _():
        for e in range(2):
            send(side, e, s1, 1).wait_send()
            send(over, e, s2, 2).wait_send()
        remote(x_ref, g_ref.at[c], full_s, full_r, c, 1 - d).wait_recv()

    for copy in forward:
        copy.wait_send()
    for slot, source in ((1, side), (2, over), (0, far)):
        theirs = part(g_ref.at[source], 1 - d)
        remote(theirs, theirs, fs.at[slot], fr.at[slot], c, 1 - d).wait_recv()


def gather_tokens(x, context):
    return pl.pallas_call(
        gather_kernel,
        out_shape=jax.ShapeDtypeStruct((context,) + x.shape, x.dtype),
        in_specs=[ANY],
        out_specs=ANY,
        scratch_shapes=[
            pltpu.SemaphoreType.DMA,
            pltpu.SemaphoreType.DMA,
            pltpu.SemaphoreType.DMA,
            pltpu.SemaphoreType.DMA((2,)),
            pltpu.SemaphoreType.DMA((2,)),
            pltpu.SemaphoreType.DMA((3,)),
            pltpu.SemaphoreType.DMA((3,)),
            pltpu.SemaphoreType.DMA((3,)),
        ],
        compiler_params=params(collective_id=0, has_side_effects=True),
    )(x)


def home_kernel(x_ref, o_ref, local, send, recv):
    c, e = coords()
    seq = sequence_of(c)
    pair = 2 * (c // 2) + e
    plane_barrier(c, e)
    for k in range(4):
        b = lax.rem(c + 3 - k, 4)
        own = jnp.logical_and(b == c, e == seq)

        @pl.when(own)
        def _():
            pltpu.make_async_copy(x_ref.at[b], o_ref.at[pair], local).start()

        @pl.when(jnp.logical_not(own))
        def _():
            remote(x_ref.at[b], o_ref.at[pair], send.at[b], recv.at[pair], b, seq).start()

    for b in range(4):
        own = jnp.logical_and(b == c, e == seq)

        @pl.when(own)
        def _():
            pltpu.make_async_copy(x_ref.at[b], o_ref.at[pair], local).wait()

        @pl.when(jnp.logical_not(own))
        def _():
            remote(x_ref.at[b], o_ref.at[pair], send.at[b], recv.at[pair], b, seq).wait_send()

    for h in range(4):
        own = jnp.logical_and(h == pair, e == seq)

        @pl.when(jnp.logical_not(own))
        def _():
            remote(x_ref.at[h], o_ref.at[h], send.at[h], recv.at[h], c, e).wait_recv()


def to_home(x, cid):
    return pl.pallas_call(
        home_kernel,
        out_shape=jax.ShapeDtypeStruct(x.shape, x.dtype),
        in_specs=[ANY],
        out_specs=ANY,
        scratch_shapes=[
            pltpu.SemaphoreType.DMA,
            pltpu.SemaphoreType.DMA((4,)),
            pltpu.SemaphoreType.DMA((4,)),
        ],
        compiler_params=params(collective_id=cid, has_side_effects=True),
    )(x)


def attention_kernel(x_ref, gain_ref, w_ref, qkv_ref, o_ref, lse_ref, act_ref, ws, vx, acc):
    length = x_ref.shape[0]
    tq, tk = 1024, 512
    c, e = coords()
    pair = 2 * (c // 2) + e
    lane = lax.broadcasted_iota(jnp.int32, (1, 128), 1)
    low = lane < 64
    width = w_ref.shape[0]
    for i in range(3):
        ws[:, 128 * i : 128 * i + 128] = w_ref[
            :, pl.ds(pl.multiple_of(i * width + pair * 128, 128), 128)
        ]

    @pl.loop(0, length // TILE)
    def _(t):
        rows = pl.ds(pl.multiple_of(t * TILE, TILE), TILE)
        x = x_ref[rows, :].astype(F32)
        inv = lax.rsqrt(jnp.mean(x * x, axis=1, keepdims=True) + NORM_EPS)
        act = (x * inv * gain_ref[...]).astype(BF)
        act_ref[rows, :] = act
        qkv = dotf(act, ws[...]).astype(BF)
        qkv_ref[rows, 0:128] = qkv[:, 0:128] * jnp.asarray(0.125, BF)
        qkv_ref[rows, 128:384] = qkv[:, 128:384]
        vt = jnp.transpose(qkv[:, 256:384].astype(F32)).astype(BF)
        for h in range(2):
            vx[h, 0:64, rows] = vt[64 * h : 64 * h + 64, :]
            vx[h, 64:80, rows] = jnp.ones((16, TILE), BF)

    def step(i, j, qs, carry, diag):
        krows = pl.ds(pl.multiple_of(j * tk, tk), tk)
        k = qkv_ref[krows, 128:256]
        out = []
        first = 0 if diag is None else diag * tk
        cols = slice(first, tq)
        for h in range(2):
            m = carry[h][:, cols]
            s = dotf(k, qs[h][cols, :], ((1,), (1,)))
            if diag is not None:
                kpos = lax.broadcasted_iota(jnp.int32, s.shape, 0)
                qpos = lax.broadcasted_iota(jnp.int32, s.shape, 1)
                s = jnp.where(kpos <= qpos, s, MASKED)
            mn = jnp.maximum(m, jnp.max(s, axis=0, keepdims=True))
            p = jnp.exp(s - mn).astype(BF)
            al = jnp.exp(m - mn)
            acc[h, :, cols] = acc[h, :, cols] * al + dotf(vx[h, :, krows], p)
            if first:
                mn = jnp.concatenate([carry[h][:, :first], mn], axis=1)
            out.append(mn)
        return tuple(out)

    @pl.loop(0, length // tq)
    def _(i):
        rows = pl.ds(pl.multiple_of(i * tq, tq), tq)
        q = qkv_ref[rows, 0:128]
        z = jnp.zeros_like(q)
        qs = [jnp.where(low, q, z), jnp.where(low, z, q)]
        acc[...] = jnp.zeros_like(acc)
        m0 = jnp.full((1, tq), MASKED, F32)
        carry = lax.fori_loop(0, i * (tq // tk), lambda j, m: step(i, j, qs, m, None), (m0, m0))
        for t in range(tq // tk):
            carry = step(i, i * (tq // tk) + t, qs, carry, t)
        parts = []
        for h in range(2):
            total = acc[h, 64:65, :]
            parts.append(acc[h, 0:64, :] / total)
            lse_ref[h : h + 1, rows] = carry[h] + jnp.log(total)
        o_ref[rows, :] = jnp.transpose(jnp.concatenate(parts, axis=0)).astype(BF)


def attention(x, gain, w):
    length = x.shape[0]
    return pl.pallas_call(
        attention_kernel,
        out_shape=(
            jax.ShapeDtypeStruct((length, 384), BF),
            jax.ShapeDtypeStruct((length, 128), BF),
            jax.ShapeDtypeStruct((2, length), F32),
            jax.ShapeDtypeStruct(x.shape, BF),
        ),
        in_specs=[VMEM] * 3,
        out_specs=(VMEM,) * 4,
        scratch_shapes=[
            pltpu.VMEM((w.shape[0], 384), BF),
            pltpu.VMEM((2, 80, length), BF),
            pltpu.VMEM((2, 80, 1024), F32),
        ],
        compiler_params=params(),
        name="attention",
    )(x, gain, w)


def back_kernel(
    planes,
    datt_ref, qkv_ref, o_ref, lse_ref, act_ref, x_ref, gain_ref, w_ref, dres_ref, gp_ref, small_ref,
    tg_ref, oq_ref, op_ref, os_ref, gg_ref,
    do, qh, dh, kh, dq, dkv, delta, dsend, dhome, gq, dall,
    wire0, got0, wire1, got1, all2, sum1, back1, slots,
    wire3, got3, sum3, got4, back4, final,
    local, dsems, drecv, hsems, hrecv,
    send0, send1, send2, recv0, recv1, recv2, ret0, ret1, ssend, srecv,
    bsend, brecv, csend, crecv, cback, fsend, frecv, gsend, grecv,
):
    z = lax.axis_index("experts")
    c, d = coords()
    seq = sequence_of(c)
    column = lax.rem(c, 2)
    pair = 2 * (c // 2) + d
    side = 2 * (c // 2) + 1 - column
    over = 2 * (1 - c // 2) + column
    far = 3 - c
    native = d == seq
    length = qkv_ref.shape[0]
    block = length // 4
    width = gain_ref.shape[1]
    tq = tk = TILE
    tiles = length // TILE
    per = block // TILE
    counts = (2, 4, planes)
    places = (d, c, z)
    axes = ("dp", "context", "experts")

    def mate(stage, k):
        return {axes[stage]: lax.rem(places[stage] + k, counts[stage])}

    barrier = pltpu.get_barrier_semaphore()
    for k in range(1, 8):
        other = lax.rem(2 * c + d + k, 8)
        pl.semaphore_signal(
            barrier, inc=1, device_id={"context": other // 2, "dp": lax.rem(other, 2)},
            device_id_type=MESH,
        )
    for k in range(1, planes):
        pl.semaphore_signal(barrier, inc=1, device_id=mate(2, k), device_id_type=MESH)
    pl.semaphore_wait(barrier, 6 + planes)

    def copy(src, dst, send, recv, stage, k):
        return pltpu.make_async_remote_copy(
            src_ref=src, dst_ref=dst, send_sem=send, recv_sem=recv,
            device_id=mate(stage, k), device_id_type=MESH,
        )

    def scatter(h, go):
        chip = chip_of(d, h // 2)
        e = h % 2
        own = jnp.logical_and(chip == c, e == d)

        @pl.when(jnp.logical_and(own, go))
        def _():
            pltpu.make_async_copy(datt_ref.at[h], do.at[c], local.at[0]).start()

        @pl.when(jnp.logical_not(own))
        def _():
            op = remote(datt_ref.at[h], do.at[c], dsems.at[h], drecv.at[c], chip, e)
            op.start() if go else op.wait_send()

    for h in range(4):
        scatter(h, True)

    low = lax.broadcasted_iota(jnp.int32, (1, 128), 1) < 64
    low_rows = lax.broadcasted_iota(jnp.int32, (128, 1), 0) < 64
    head_sum = (
        lax.broadcasted_iota(jnp.int32, (8, 128), 1) // 64
        == lax.broadcasted_iota(jnp.int32, (8, 128), 0)
    ).astype(F32)

    @pl.loop(0, tiles)
    def _(t):
        rows = pl.ds(pl.multiple_of(t * TILE, TILE), TILE)
        q = qkv_ref[rows, 0:128]
        zero = jnp.zeros_like(q)
        qh[0, rows, :] = jnp.where(low, q, zero)
        qh[1, rows, :] = jnp.where(low, zero, q)
        kt = jnp.transpose(qkv_ref[rows, 128:256].astype(F32)).astype(BF)
        zt = jnp.zeros_like(kt)
        kh[0, :, rows] = jnp.where(low_rows, kt, zt)
        kh[1, :, rows] = jnp.where(low_rows, zt, kt)
        dq[:, rows] = jnp.zeros((128, TILE), F32)
        dkv[rows, :] = jnp.zeros((TILE, 256), F32)

    gq[...] = jnp.zeros_like(gq)

    width_half = width // 2
    eighth = width_half // 4

    def small_start(stage, value):
        slots[stage, places[stage]] = value
        own = slots.at[stage, places[stage]]
        for k in range(1, counts[stage]):
            copy(own, own, ssend.at[stage, k - 1], srecv.at[stage, k - 1], stage, k).start()

    def small_sum(stage):
        own = slots.at[stage, places[stage]]
        for k in range(1, counts[stage]):
            copy(own, own, ssend.at[stage, k - 1], srecv.at[stage, k - 1], stage, k).wait()
        value = slots[stage, 0]
        for k in range(1, counts[stage]):
            value = value + slots[stage, k]
        return value

    def stage0():
        return copy(wire0, got0, send0, recv0, 0, 1)

    def stage1(k):
        rows = pl.ds(lax.rem(c + k, 4) * eighth, eighth)
        return copy(wire1.at[rows], got1.at[k - 1], send1.at[k - 1], recv1.at[k - 1], 1, k)

    def stage2(k):
        return copy(all2.at[z], all2.at[z], send2.at[k - 1], recv2.at[k - 1], 2, k)

    own1 = pl.ds(pl.multiple_of(c * eighth, eighth), eighth)

    def stage4(k):
        return copy(back1.at[d, own1], back1.at[d, own1], send1.at[k - 1], ret1.at[k - 1], 1, k)

    def stage5():
        return copy(back1.at[d], back1.at[d], send0, ret0, 0, 1)

    def early(t):
        @pl.when(t == 0)
        def _():
            wire0[...] = gp_ref[pl.ds(pl.multiple_of((1 - d) * width_half, width_half), width_half), :].astype(BF)
            stage0().start()
            small_start(0, small_ref[...])

        @pl.when(t == 1)
        def _():
            stage0().wait()
            mine = gp_ref[pl.ds(pl.multiple_of(d * width_half, width_half), width_half), :] + got0[...].astype(F32)
            sum1[...] = mine
            wire1[...] = mine.astype(BF)
            for k in (2, 1, 3):
                stage1(k).start()
            small_start(1, small_sum(0))

        @pl.when(t == 2)
        def _():
            for k in range(1, 4):
                stage1(k).wait()
            mine = sum1[own1, :]
            for k in range(3):
                mine = mine + got1[k].astype(F32)
            all2[z] = mine.astype(BF)
            for k in range(1, planes):
                stage2(k).start()
            small_start(2, small_sum(1))

        @pl.when(t == 3)
        def _():
            for k in range(1, planes):
                stage2(k).wait()
            mine = all2[0].astype(F32)
            for k in range(1, planes):
                mine = mine + all2[k].astype(F32)
            back1[d, own1, :] = mine.astype(BF)
            for k in (2, 1, 3):
                stage4(k).start()
            os_ref[...] = small_sum(2)

        @pl.when(t == 4)
        def _():
            for k in range(1, 4):
                stage4(k).wait()
            stage5().start()

        @pl.when(t == 5)
        def _():
            stage5().wait()
            for i in range(2):
                op_ref[i * width_half : (i + 1) * width_half, :] = back1[i].astype(F32)

    for source in (c, side, over, far):
        if source is c:
            @pl.when(native)
            def _():
                pltpu.make_async_copy(datt_ref.at[0], do.at[c], local.at[0]).wait()

            @pl.when(jnp.logical_not(native))
            def _():
                remote(do.at[c], do.at[c], dsems.at[0], drecv.at[c], c, d).wait_recv()
        else:
            remote(do.at[source], do.at[source], dsems.at[0], drecv.at[source], c, d).wait_recv()

        @pl.loop(0, per)
        def _(t):
            part = pl.ds(pl.multiple_of(t * TILE, TILE), TILE)
            rows = pl.ds(pl.multiple_of(source * block + t * TILE, TILE), TILE)
            g = do[source, part, :]
            zero = jnp.zeros_like(g)
            dh[0, rows, :] = jnp.where(low, g, zero)
            dh[1, rows, :] = jnp.where(low, zero, g)
            product = g.astype(F32) * o_ref[rows, :].astype(F32)
            delta[:, rows] = dotf(
                head_sum, product, ((1,), (1,)), precision=lax.Precision.HIGHEST
            )

    def step(i, j, masked):
        qrows = pl.ds(pl.multiple_of(i * tq, tq), tq)
        krows = pl.ds(pl.multiple_of(j * tk, tk), tk)
        k = qkv_ref[krows, 128:256]
        v = qkv_ref[krows, 256:384]
        dk = dv = dqt = 0.0
        for h in range(2):
            s = dotf(k, qh[h, qrows, :], ((1,), (1,)))
            p = jnp.exp(s - lse_ref[h : h + 1, qrows])
            if masked:
                kpos = lax.broadcasted_iota(jnp.int32, (tk, tq), 0)
                qpos = lax.broadcasted_iota(jnp.int32, (tk, tq), 1)
                p = jnp.where(kpos <= qpos, p, 0.0)
            dp = dotf(v, dh[h, qrows, :], ((1,), (1,)))
            ds = (p * (dp - delta[h : h + 1, qrows])).astype(BF)
            dv = dv + dotf(p.astype(BF), dh[h, qrows, :])
            dk = dk + dotf(ds, qh[h, qrows, :])
            dqt = dqt + dotf(kh[h, :, krows], ds)
        dq[:, qrows] = dq[:, qrows] + dqt
        dkv[krows, 0:128] = dkv[krows, 0:128] + dk
        dkv[krows, 128:256] = dkv[krows, 128:256] + dv

    def send_home(b, go):
        own = jnp.logical_and(b == c, native)

        @pl.when(own)
        def _():
            op = pltpu.make_async_copy(dsend.at[b], dhome.at[pair], local.at[1])
            op.start() if go else op.wait()

        @pl.when(jnp.logical_not(own))
        def _():
            op = remote(dsend.at[b], dhome.at[pair], hsems.at[b], hrecv.at[pair], b, seq)
            op.start() if go else op.wait_send()

    @pl.loop(0, tiles)
    def _(t):
        early(t)
        diagonal = jnp.where(d == 0, t, tiles - 1 - t)
        step(diagonal, diagonal, True)

        @pl.loop(1, tiles - t)
        def _(u):
            step(
                jnp.where(d == 0, t + u, tiles - 1 - t),
                jnp.where(d == 0, t, tiles - 1 - t - u),
                False,
            )

        @pl.when(lax.rem(t, per) == per - 1)
        def _():
            b = diagonal // per
            for half in range(per):
                rows = pl.ds(pl.multiple_of(b * block + half * TILE, TILE), TILE)
                part = slice(half * TILE, half * TILE + TILE)
                dsend[b, part, 0:128] = (jnp.transpose(dq[:, rows]) * 0.125).astype(BF)
                dsend[b, part, 128:384] = dkv[rows, :].astype(BF)
            for k in range(4):
                @pl.when(b == k)
                def _():
                    send_home(k, True)
            rows = pl.ds(pl.multiple_of(b * block, block), block)
            gq[...] = gq[...] + dotf(act_ref[rows, :], dsend[b], ((0,), (0,)))

    rest = gq.shape[0] // 2
    bit = rest // planes

    def next0():
        return remote(wire3, got3, bsend, brecv, side, d)

    def next1(k):
        rows = pl.ds(lax.rem(z + k, planes) * bit, bit)
        return copy(wire3.at[rows], got4.at[k - 1], csend.at[k - 1], crecv.at[k - 1], 2, k)

    own3 = pl.ds(pl.multiple_of(z * bit, bit), bit)

    def next2(k):
        return copy(back4.at[own3], back4.at[own3], csend.at[k - 1], cback.at[k - 1], 2, k)

    def next3(k):
        return copy(final.at[c, d], final.at[c, d], fsend.at[k - 1], frecv.at[k - 1], 1, k)

    def next4(k):
        chip = lax.rem(c + k, 4)
        return copy(final.at[chip, d], final.at[chip, d], gsend.at[k], grecv.at[chip], 0, 1)

    wire3[...] = gq[pl.ds(pl.multiple_of((1 - column) * rest, rest), rest), :].astype(BF)
    next0().start()
    for h in range(4):
        scatter(h, False)
    next0().wait()
    mine = gq[pl.ds(pl.multiple_of(column * rest, rest), rest), :] + got3[...].astype(F32)
    sum3[...] = mine
    wire3[...] = mine.astype(BF)
    for k in range(1, planes):
        next1(k).start()
    for k in range(1, planes):
        next1(k).wait()
    mine = sum3[own3, :]
    for k in range(planes - 1):
        mine = mine + got4[k].astype(F32)
    back4[own3, :] = mine.astype(BF)
    for k in range(1, planes):
        next2(k).start()

    for b in range(4):
        send_home(b, False)
    for h in range(4):
        own = jnp.logical_and(h == pair, native)

        @pl.when(jnp.logical_not(own))
        def _():
            remote(dhome.at[h], dhome.at[h], hsems.at[h], hrecv.at[h], c, d).wait_recv()

        for i in range(3):
            first = i * width + 128 * h
            dall[:, first : first + 128] = dhome[h, :, 128 * i : 128 * i + 128]

    def input_rows(first, last):
        @pl.loop(first, last)
        def _(t):
            rows = pl.ds(pl.multiple_of(t * 256, 256), 256)
            x = x_ref[rows, :].astype(F32)
            inv = lax.rsqrt(jnp.mean(x * x, axis=1, keepdims=True) + NORM_EPS)
            normed = x * inv
            scaled = dotf(dall[rows, :], w_ref[...], ((1,), (1,))) * gain_ref[...]
            inner = jnp.mean(scaled * normed, axis=1, keepdims=True)
            tg_ref[rows, :] = dres_ref[rows, :] + inv * (scaled - normed * inner)

    count = x_ref.shape[0] // 256
    input_rows(0, count // 2)
    for k in range(1, planes):
        next2(k).wait()
    final[c, d] = back4[...]
    for k in (2, 1, 3):
        next3(k).start()
    next4(0).start()
    input_rows(count // 2, count)
    for k in range(1, 4):
        next3(k).wait_send()
    for k in (1, 3, 2):
        chip = lax.rem(c + 4 - k, 4)
        copy(final.at[chip, d], final.at[chip, d], fsend.at[k - 1], frecv.at[k - 1], 1, k).wait_recv()
        next4(4 - k).start()
    for k in range(4):
        next4(k).wait_send()
    for chip in range(4):
        copy(final.at[chip, 1 - d], final.at[chip, 1 - d], gsend.at[chip], grecv.at[chip], 0, 1).wait_recv()
    for chip in range(4):
        for e in range(2):
            rows = slice((chip % 2) * rest, (chip % 2 + 1) * rest)
            for i in range(3):
                first = i * width + (2 * (chip // 2) + e) * 128
                oq_ref[rows, first : first + 128] = final[chip, e, :, 128 * i : 128 * i + 128].astype(F32)
    weighted = oq_ref[...] * w_ref[...].astype(F32)
    gg_ref[...] = (
        dotf(jnp.ones((8, weighted.shape[1]), F32), weighted, ((1,), (1,)), precision=lax.Precision.HIGHEST)
        / gain_ref[...]
    )


def back_pass(d_att, qkv, o, lse, act, x, gain, w, d_res, g_proj, small, planes):
    length = qkv.shape[0]
    count, width = x.shape
    half = width // 2
    eighth = half // 4
    rest = width // 2
    most = max(4, planes)
    dma = pltpu.SemaphoreType.DMA
    return pl.pallas_call(
        functools.partial(back_kernel, planes),
        out_shape=(
            jax.ShapeDtypeStruct((count, width), F32),
            jax.ShapeDtypeStruct((width, 3 * width), F32),
            jax.ShapeDtypeStruct((width, width), F32),
            jax.ShapeDtypeStruct(small.shape, F32),
            jax.ShapeDtypeStruct((8, width), F32),
        ),
        in_specs=[VMEM] * 11,
        out_specs=(VMEM,) * 5,
        scratch_shapes=[
            pltpu.VMEM((4, count, 128), BF),
            pltpu.VMEM((2, length, 128), BF),
            pltpu.VMEM((2, length, 128), BF),
            pltpu.VMEM((2, 128, length), BF),
            pltpu.VMEM((128, length), F32),
            pltpu.VMEM((length, 256), F32),
            pltpu.VMEM((8, length), F32),
            pltpu.VMEM((4, count, 384), BF),
            pltpu.VMEM((4, count, 384), BF),
            pltpu.VMEM((width, 384), F32),
            pltpu.VMEM((count, 3 * width), BF),
            pltpu.VMEM((half, width), BF),
            pltpu.VMEM((half, width), BF),
            pltpu.VMEM((half, width), BF),
            pltpu.VMEM((3, eighth, width), BF),
            pltpu.VMEM((planes, eighth, width), BF),
            pltpu.VMEM((half, width), F32),
            pltpu.VMEM((2, half, width), BF),
            pltpu.VMEM((3, most) + small.shape, F32),
            pltpu.VMEM((rest, 384), BF),
            pltpu.VMEM((rest, 384), BF),
            pltpu.VMEM((rest, 384), F32),
            pltpu.VMEM((planes - 1, rest // planes, 384), BF),
            pltpu.VMEM((rest, 384), BF),
            pltpu.VMEM((4, 2, rest, 384), BF),
            dma((2,)), dma((4,)), dma((4,)), dma((4,)), dma((4,)),
            dma, dma((3,)), dma((planes - 1,)),
            dma, dma((3,)), dma((planes - 1,)),
            dma, dma((3,)),
            dma((3, most - 1)), dma((3, most - 1)),
            dma, dma, dma((planes - 1,)), dma((planes - 1,)), dma((planes - 1,)),
            dma((3,)), dma((3,)), dma((4,)), dma((4,)),
        ],
        compiler_params=params(collective_id=2, has_side_effects=True),
        name="back_pass",
    )(d_att, qkv, o, lse, act, x, gain, w, d_res, g_proj, small)


def mix_kernel(
    stride, capacity, local, choices,
    x_ref, att_ref, wo_ref, gain_ref, router_ref, slot_ref, pair_ref, gout_ref,
    res_ref, mix_ref, wts_ref, place_ref, send_ref,
    att,
):
    tokens = x_ref.shape[0]
    pairs = pair_ref.shape[1]
    experts = router_ref.shape[1]
    members = tokens * choices // pairs
    for h in range(4):
        att[:, 128 * h : 128 * h + 128] = att_ref[h]

    @pl.loop(0, tokens // 256)
    def _(t):
        rows = pl.ds(pl.multiple_of(t * 256, 256), 256)
        res = x_ref[rows, :].astype(F32) + dotf(att[rows, :], wo_ref[...])
        inv = lax.rsqrt(jnp.mean(res * res, axis=1, keepdims=True) + NORM_EPS)
        res_ref[rows, :] = res
        mix_ref[rows, :] = (res * inv * gain_ref[...]).astype(BF)

    routes = pair_ref[0:1, :]
    order = pair_ref[1:2, :]
    eye = lax.broadcasted_iota(jnp.int32, (pairs, pairs), 0) == lax.broadcasted_iota(
        jnp.int32, (pairs, pairs), 1
    )
    zero = jnp.zeros((pairs, pairs), F32)

    def as_column(row):
        return jnp.sum(jnp.where(eye, row.astype(F32), zero), axis=1, keepdims=True)

    route_col = as_column(routes)
    order_col = as_column(order)
    ahead = jnp.logical_and(route_col == routes.astype(F32), order_col < order.astype(F32))
    rank = jnp.sum(ahead.astype(F32), axis=0, keepdims=True).astype(jnp.int32)
    slots = place_ref.shape[0]
    block = lax.div(routes, local)
    place = block * stride + (routes - block * local) * capacity + rank
    place = jnp.where(rank < capacity, place, slots)
    spread = (lax.broadcasted_iota(jnp.int32, (slots, pairs), 0) == place).astype(BF)
    place_ref[...] = spread

    pick = (lax.broadcasted_iota(jnp.int32, (experts, pairs), 0) == routes).astype(F32)
    columns = dotf(router_ref[...].astype(F32), pick).astype(BF)
    chosen = dotf(columns, mix_ref[...], ((0,), (1,)))
    group = lax.broadcasted_iota(jnp.int32, (pairs, 1), 0) // choices
    member = group == slot_ref[...] // members
    chosen = jnp.where(member, chosen, MASKED)
    peak = jnp.max(chosen, axis=1, keepdims=True)
    weight = jnp.where(member, jnp.exp(chosen - peak), 0.0)
    weight = weight / jnp.sum(weight, axis=1, keepdims=True)
    wts_ref[...] = weight
    low = weight.astype(BF)
    width = mix_ref.shape[1]
    mixed = dotf(low, mix_ref[...]).astype(BF)
    send_ref[:, 0:width] = dotf(spread, mixed).astype(BF)
    dy = dotf(low, gout_ref[...]).astype(BF)
    send_ref[:, width:] = dotf(spread, dy).astype(BF)


def gelu_parts(x):
    scale = np.float32(np.sqrt(2.0 / np.pi))
    square = x * x
    t = jnp.tanh(scale * (x + np.float32(0.044715) * (square * x)))
    half = 0.5 * (1.0 + t)
    slope = half + (0.5 * x) * (1.0 - t * t) * (
        scale * (1.0 + np.float32(3 * 0.044715) * square)
    )
    return x * half, slope


def expert_kernel(steps, recv_ref, pick_ref, win_ref, wout_ref, rows_ref, ret_ref, y, dx):
    e = pl.program_id(0)
    f = pl.program_id(1)
    width = win_ref.shape[1]

    @pl.when(f == 0)
    def _():
        rows_ref[0] = dotf(pick_ref[0], recv_ref[...]).astype(BF)
        y[...] = jnp.zeros_like(y)
        dx[...] = jnp.zeros_like(dx)

    @pl.when(jnp.logical_and(e == 0, f == 0))
    def _():
        ret_ref[...] = jnp.zeros_like(ret_ref)

    x = rows_ref[0, :, 0:width]
    dy = rows_ref[0, :, width:]
    hidden, slope = gelu_parts(dotf(x, win_ref[0]))
    y[...] += dotf(hidden.astype(BF), wout_ref[0])
    d_pre = (dotf(dy, wout_ref[0], ((1,), (1,))) * slope).astype(BF)
    dx[...] += dotf(d_pre, win_ref[0], ((1,), (1,)))

    @pl.when(f == steps - 1)
    def _():
        both = jnp.concatenate([y[...].astype(BF), dx[...].astype(BF)], axis=1)
        ret_ref[...] += dotf(pick_ref[0], both, ((0,), (0,))).astype(BF)


def expert_rows(recv, pick, w_in, w_out):
    local, count, total = pick.shape
    _, width, hidden = w_in.shape
    chunk = 512
    steps = hidden // chunk
    return pl.pallas_call(
        functools.partial(expert_kernel, steps),
        grid=(local, steps),
        out_shape=(
            jax.ShapeDtypeStruct((local, count, 2 * width), BF),
            jax.ShapeDtypeStruct((total, 2 * width), BF),
        ),
        in_specs=[
            pl.BlockSpec((total, 2 * width), lambda e, f: (0, 0)),
            pl.BlockSpec((1, count, total), lambda e, f: (e, 0, 0)),
            pl.BlockSpec((1, width, chunk), lambda e, f: (e, 0, f)),
            pl.BlockSpec((1, chunk, width), lambda e, f: (e, f, 0)),
        ],
        out_specs=(
            pl.BlockSpec((1, count, 2 * width), lambda e, f: (e, 0, 0)),
            pl.BlockSpec((total, 2 * width), lambda e, f: (0, 0)),
        ),
        scratch_shapes=[pltpu.VMEM((count, width), F32), pltpu.VMEM((count, width), F32)],
        compiler_params=params(),
        name="expert_rows",
    )(recv, pick, w_in, w_out)


def expert_grad_kernel(rows_ref, win_ref, wout_ref, gin_ref, gout_ref, x, dy):
    width = win_ref.shape[1]
    copies, _, count, _ = rows_ref.shape

    @pl.when(pl.program_id(1) == 0)
    def _():
        for k in range(copies):
            x[k * count : (k + 1) * count, :] = rows_ref[k, 0, :, 0:width]
            dy[k * count : (k + 1) * count, :] = rows_ref[k, 0, :, width:]

    hidden, slope = gelu_parts(dotf(x[...], win_ref[0]))
    d_pre = (dotf(dy[...], wout_ref[0], ((1,), (1,))) * slope).astype(BF)
    gin_ref[0] = dotf(x[...], d_pre, ((0,), (0,)))
    gout_ref[0] = dotf(hidden.astype(BF), dy[...], ((0,), (0,)))


def expert_grads(rows, w_in, w_out):
    copies, local, count, double = rows.shape
    _, width, hidden = w_in.shape
    chunk = 256
    return pl.pallas_call(
        expert_grad_kernel,
        grid=(local, hidden // chunk),
        out_shape=(
            jax.ShapeDtypeStruct(w_in.shape, F32),
            jax.ShapeDtypeStruct(w_out.shape, F32),
        ),
        in_specs=[
            pl.BlockSpec((copies, 1, count, double), lambda e, f: (0, e, 0, 0)),
            pl.BlockSpec((1, width, chunk), lambda e, f: (e, 0, f)),
            pl.BlockSpec((1, chunk, width), lambda e, f: (e, f, 0)),
        ],
        out_specs=(
            pl.BlockSpec((1, width, chunk), lambda e, f: (e, 0, f)),
            pl.BlockSpec((1, chunk, width), lambda e, f: (e, f, 0)),
        ),
        scratch_shapes=[
            pltpu.VMEM((copies * count, width), BF),
            pltpu.VMEM((copies * count, width), BF),
        ],
        compiler_params=params(),
        cost_estimate=pl.CostEstimate(
            flops=8 * copies * local * count * width * hidden,
            bytes_accessed=12 * local * width * hidden,
            transcendentals=copies * local * count * hidden,
        ),
        name="expert_grads",
    )(rows, w_in, w_out)


def unmix_kernel(
    choices,
    res_ref, mix_ref, wts_ref, place_ref, ret_ref, gout_ref, att_ref, wo_ref, gain_ref, router_ref,
    pair_ref,
    out_ref, dres_ref, datt_ref, gproj_ref, small_ref,
    att, dproj, back,
):
    tokens, width = res_ref.shape
    experts = router_ref.shape[1]
    pairs = pair_ref.shape[1]
    rows_back = dotf(place_ref[...], ret_ref[...], ((0,), (0,))).astype(BF)
    y = rows_back[:, 0:width]
    dm = rows_back[:, width:]
    weight = wts_ref[...]
    low = weight.astype(BF)
    dw = dotf(y, gout_ref[...], ((1,), (1,))) + dotf(dm, mix_ref[...], ((1,), (1,)))
    d_chosen = weight * (dw - jnp.sum(weight * dw, axis=1, keepdims=True))
    pick = (
        lax.broadcasted_iota(jnp.int32, (experts, pairs), 0) == pair_ref[0:1, :]
    ).astype(BF)
    d_logits = dotf(pick, d_chosen.astype(BF)).astype(BF)
    small_ref[0:experts, :] = dotf(d_logits, mix_ref[...])
    small_ref[experts:, :] = jnp.zeros((small_ref.shape[0] - experts, width), F32)
    spare = back.shape[0] - pairs - experts
    back[0:pairs, :] = low
    back[pairs : pairs + experts, :] = d_logits
    if spare:
        back[pairs + experts :, :] = jnp.zeros((spare, tokens), BF)
    router_t = jnp.transpose(
        jnp.concatenate(
            [router_ref[...].astype(F32), jnp.zeros((width, 128 - experts), F32)], axis=1
        )
    ).astype(BF)[0 : back.shape[0] - pairs, :]
    for h in range(4):
        att[:, 128 * h : 128 * h + 128] = att_ref[h]
    rhs = jnp.concatenate([dm, router_t], axis=0)
    gain_grad = jnp.zeros((1, width), F32)
    for t in range(tokens // 256):
        rows = slice(t * 256, t * 256 + 256)
        res = res_ref[rows, :]
        combined = dotf(low[:, rows], y, ((0,), (0,)))
        out_ref[rows, :] = (res + combined).astype(BF)
        d_mix = dotf(back[:, rows], rhs, ((0,), (0,)))
        inv = lax.rsqrt(jnp.mean(res * res, axis=1, keepdims=True) + NORM_EPS)
        normed = res * inv
        scaled = d_mix * gain_ref[...]
        gain_grad = gain_grad + jnp.sum(d_mix * normed, axis=0, keepdims=True)
        inner = jnp.mean(scaled * normed, axis=1, keepdims=True)
        d_res = gout_ref[rows, :].astype(F32) + inv * (scaled - normed * inner)
        dres_ref[rows, :] = d_res
        d_low = d_res.astype(BF)
        dproj[rows, :] = d_low
        d_att = dotf(d_low, wo_ref[...], ((1,), (1,))).astype(BF)
        for h in range(4):
            datt_ref[h, rows, :] = d_att[:, 128 * h : 128 * h + 128]
    small_ref[experts : experts + 1, :] = gain_grad
    gproj_ref[...] = dotf(att[...], dproj[...], ((0,), (0,)))


def pick_rows(sources, local, capacity, stride):
    pick = np.zeros((local, sources * capacity, sources * stride), np.float32)
    for e in range(local):
        for r in range(sources * capacity):
            pick[e, r, (r // capacity) * stride + e * capacity + r % capacity] = 1.0
    return pick


def per_device(
    planes,
    tokens,
    attn_gain,
    mix_gain,
    query_key_value_weight,
    output_weight,
    router_weight,
    w_in,
    w_exp_out,
    out_grad,
    group_slot,
    group_routes,
    route_order,
):
    x = tokens[0]
    gout = out_grad[0]
    count, width = x.shape
    groups, choices = group_routes.shape
    pairs = groups * choices
    experts = router_weight.shape[1]
    local = w_in.shape[0]
    sources = experts // local
    capacity = 5 * groups * choices // (4 * experts)
    stride = -(-local * capacity // 16) * 16
    slots = sources * stride
    small_rows = -(-(experts + 2) // 8) * 8
    gain_one = attn_gain.reshape(1, width)
    gain_two = mix_gain.reshape(1, width)
    pair_table = jnp.stack([group_routes.reshape(-1), route_order.reshape(-1)])

    sequence = gather_tokens(x, 4).reshape(4 * count, width)
    qkv, o, lse, act = attention(sequence, gain_one, query_key_value_weight)
    att = to_home(o.reshape(4, count, 128), 1)

    res, mix, weights, place, send = pl.pallas_call(
        functools.partial(mix_kernel, stride, capacity, local, choices),
        out_shape=(
            jax.ShapeDtypeStruct((count, width), F32),
            jax.ShapeDtypeStruct((count, width), BF),
            jax.ShapeDtypeStruct((pairs, count), F32),
            jax.ShapeDtypeStruct((slots, pairs), BF),
            jax.ShapeDtypeStruct((slots, 2 * width), BF),
        ),
        in_specs=[VMEM] * 8,
        out_specs=(VMEM,) * 5,
        scratch_shapes=[pltpu.VMEM((count, width), BF)],
        compiler_params=params(),
        name="mix",
    )(x, att, output_weight, gain_two, router_weight, group_slot, pair_table, gout)

    recv = lax.all_to_all(
        send.reshape(sources, stride, 2 * width), "experts", split_axis=0, concat_axis=0, tiled=True
    ).reshape(slots, 2 * width)
    pick = jnp.asarray(pick_rows(sources, local, capacity, stride), BF)
    rows, ret = expert_rows(recv, pick, w_in, w_exp_out)
    ret = lax.all_to_all(
        ret.reshape(sources, stride, 2 * width), "experts", split_axis=0, concat_axis=0, tiled=True
    ).reshape(slots, 2 * width)
    all_rows = lax.all_gather(rows, ("context", "dp"), axis=0)

    layer_out, d_res, d_att, g_proj, small = pl.pallas_call(
        functools.partial(unmix_kernel, choices),
        out_shape=(
            jax.ShapeDtypeStruct((count, width), BF),
            jax.ShapeDtypeStruct((count, width), F32),
            jax.ShapeDtypeStruct((4, count, 128), BF),
            jax.ShapeDtypeStruct((width, width), F32),
            jax.ShapeDtypeStruct((small_rows, width), F32),
        ),
        in_specs=[VMEM] * 11,
        out_specs=(VMEM,) * 5,
        scratch_shapes=[
            pltpu.VMEM((count, width), BF),
            pltpu.VMEM((count, width), BF),
            pltpu.VMEM((pairs + -(-experts // 16) * 16, count), BF),
        ],
        compiler_params=params(),
        name="unmix",
    )(
        res, mix, weights, place, ret, gout, att, output_weight, gain_two, router_weight, pair_table
    )

    token_grad, qkv_grad, proj_grad, small, g_one = back_pass(
        d_att, qkv, o, lse, act, x, gain_one, query_key_value_weight, d_res, g_proj, small, planes
    )
    g_in, g_out = expert_grads(all_rows, w_in, w_exp_out)
    return (
        layer_out[None],
        token_grad[None],
        g_one[0],
        small[experts],
        qkv_grad,
        proj_grad,
        jnp.transpose(small[:experts]),
        g_in,
        g_out,
    )


def solution(mesh):
    token_spec = P(("experts", "dp"), "context", None)
    pair_spec = P(("experts", "context", "dp"), None)
    expert_spec = P("experts", None, None)
    return jax.shard_map(
        functools.partial(per_device, mesh.shape["experts"]),
        mesh=mesh,
        in_specs=(
            token_spec, P(), P(), P(), P(), P(), expert_spec, expert_spec, token_spec,
            P(("experts", "dp"), "context"), pair_spec, pair_spec,
        ),
        out_specs=(
            token_spec, token_spec, P(), P(), P(), P(), P(), expert_spec, expert_spec,
        ),
        check_vma=False,
    )
```

```python
import functools

import jax
import jax.numpy as jnp
import numpy as np
from jax import lax
from jax.experimental import pallas as pl
from jax.experimental.pallas import tpu as pltpu
from jax.sharding import PartitionSpec as P

HEADS = 8
NORM_EPS = 1e-05
MASKED = -1e30
F32 = jnp.float32
BF = jnp.bfloat16
MESH = pl.DeviceIdType.MESH
VMEM = pl.BlockSpec(memory_space=pltpu.VMEM)
ANY = pl.BlockSpec(memory_space=pl.ANY)
LIMIT = 60 << 20
TILE = 512


def dotf(a, b, dims=((1,), (0,)), **kw):
    return lax.dot_general(a, b, (dims, ((), ())), preferred_element_type=F32, **kw)


def params(**kw):
    return pltpu.CompilerParams(vmem_limit_bytes=LIMIT, **kw)


def sequence_of(c):
    return lax.rem(lax.rem(c, 2) + c // 2, 2)


def chip_of(seq, rank):
    return 2 * rank + lax.rem(seq + rank, 2)


def coords():
    return lax.axis_index("context"), lax.axis_index("dp")


def plane_barrier(c, d):
    barrier = pltpu.get_barrier_semaphore()
    for k in range(1, 8):
        other = lax.rem(2 * c + d + k, 8)
        pl.semaphore_signal(
            barrier,
            inc=1,
            device_id={"context": other // 2, "dp": lax.rem(other, 2)},
            device_id_type=MESH,
        )
    pl.semaphore_wait(barrier, 7)


def remote(src, dst, send_sem, recv_sem, context, dp):
    return pltpu.make_async_remote_copy(
        src_ref=src,
        dst_ref=dst,
        send_sem=send_sem,
        recv_sem=recv_sem,
        device_id={"context": context, "dp": dp},
        device_id_type=MESH,
    )


def forward_kernel(
    x_ref, gain_ref, w_ref,
    att_ref, qkv_out, o_out, act_out, lse_ref,
    g, ws, qkv, qh, vx, acc, peak, o, act,
    local, full_s, full_r, s1, s2, hr, fs, fr, hsems, hrecv, outs,
):
    c, d = coords()
    seq = sequence_of(c)
    column = lax.rem(c, 2)
    row = c // 2
    pair = 2 * row + d
    native = d == seq
    block, width = x_ref.shape
    half = block // 2

    def at_phase(p):
        return 2 * lax.rem(row + p // 2, 2) + lax.rem(column + lax.rem(p, 2), 2)

    side, over, far = at_phase(1), at_phase(2), at_phase(3)
    plane_barrier(c, d)

    def part(ref, e):
        return ref.at[pl.ds(e * half, half)]

    def send(target, e, sem, slot):
        return remote(part(x_ref, e), part(g.at[c], e), sem.at[e], hr.at[slot], target, e)

    def whole():
        return remote(x_ref, g.at[c], full_s, full_r, c, 1 - d)

    def keep():
        return pltpu.make_async_copy(x_ref, g.at[c], local.at[0])

    def pass_on(slot, source, e):
        mine = part(g.at[source], e)
        return remote(mine, mine, fs.at[slot], fr.at[slot], c, 1 - d)

    @pl.when(native)
    def _():
        keep().start()
        whole().start()

    @pl.when(jnp.logical_not(native))
    def _():
        for e in range(2):
            send(side, e, s1, 1).start()
            send(over, e, s2, 2).start()

    low = lax.broadcasted_iota(jnp.int32, (1, 128), 1) < 64
    for i in range(3):
        ws[:, 128 * i : 128 * i + 128] = w_ref[
            :, pl.ds(pl.multiple_of(i * width + pair * 128, 128), 128)
        ]

    def project(b):
        @pl.loop(0, block // TILE)
        def _(t):
            rows = pl.ds(pl.multiple_of(b * block + t * TILE, TILE), TILE)
            x = g[b, pl.ds(pl.multiple_of(t * TILE, TILE), TILE), :].astype(F32)
            inv = lax.rsqrt(jnp.mean(x * x, axis=1, keepdims=True) + NORM_EPS)
            low_act = (x * inv * gain_ref[...]).astype(BF)
            act[rows, :] = low_act
            value = dotf(low_act, ws[...]).astype(BF)
            q = value[:, 0:128] * jnp.asarray(0.125, BF)
            zero = jnp.zeros_like(q)
            qkv[rows, 0:128] = q
            qkv[rows, 128:384] = value[:, 128:384]
            qh[0, rows, :] = jnp.where(low, q, zero)
            qh[1, rows, :] = jnp.where(low, zero, q)
            vt = jnp.transpose(value[:, 256:384].astype(F32)).astype(BF)
            for h in range(2):
                vx[h, 0:64, rows] = vt[64 * h : 64 * h + 64, :]
                vx[h, 64:80, rows] = jnp.ones((16, TILE), BF)
                acc[h, :, rows] = jnp.zeros((80, TILE), F32)
                peak[h : h + 1, rows] = jnp.full((1, TILE), MASKED, F32)
        rows = pl.ds(pl.multiple_of(b * block, block), block)
        pltpu.make_async_copy(qkv.at[rows], qkv_out.at[rows], outs.at[0, b]).start()
        pltpu.make_async_copy(act.at[rows], act_out.at[rows], outs.at[1, b]).start()

    def attend(qb, kb, first_key, first_query, keys, masked):
        count = block - first_query
        krows = pl.ds(pl.multiple_of(kb * block + first_key, keys), keys)
        qrows = pl.ds(pl.multiple_of(qb * block + first_query, 256), count)
        k = qkv[krows, 128:256]
        scores = [dotf(k, qh[h, qrows, :], ((1,), (1,))) for h in range(2)]
        for h in range(2):
            s = scores[h]
            if masked:
                kpos = lax.broadcasted_iota(jnp.int32, s.shape, 0)
                qpos = lax.broadcasted_iota(jnp.int32, s.shape, 1)
                s = jnp.where(kpos <= qpos, s, MASKED)
            m = peak[h : h + 1, qrows]
            mn = jnp.maximum(m, jnp.max(s, axis=0, keepdims=True))
            p = jnp.exp(s - mn).astype(BF)
            al = jnp.exp(m - mn)
            acc[h, :, qrows] = acc[h, :, qrows] * al + dotf(vx[h, :, krows], p)
            peak[h : h + 1, qrows] = mn

    def home(b):
        rows = pl.ds(pl.multiple_of(b * block, block), block)
        return remote(o.at[rows], att_ref.at[pair], hsems.at[b], hrecv.at[pair], b, seq)

    def home_own():
        rows = pl.ds(pl.multiple_of(c * block, block), block)
        return pltpu.make_async_copy(o.at[rows], att_ref.at[pair], local.at[1])

    def finish(b):
        @pl.loop(0, block // TILE)
        def _(t):
            rows = pl.ds(pl.multiple_of(b * block + t * TILE, TILE), TILE)
            parts = []
            for h in range(2):
                total = acc[h, 64:65, rows]
                parts.append(acc[h, 0:64, rows] / total)
                lse_ref[h : h + 1, rows] = peak[h : h + 1, rows] + jnp.log(total)
            o[rows, :] = jnp.transpose(jnp.concatenate(parts, axis=0)).astype(BF)
        own = jnp.logical_and(b == c, native)

        @pl.when(own)
        def _():
            home_own().start()

        @pl.when(jnp.logical_not(own))
        def _():
            home(b).start()

        rows = pl.ds(pl.multiple_of(b * block, block), block)
        pltpu.make_async_copy(o.at[rows], o_out.at[rows], outs.at[2, b]).start()

    last_phase = []
    for b in range(4):
        phase = at_phase(b)
        last_phase.append(phase if b == 0 else jnp.maximum(last_phase[-1], phase))

    def complete(b, p):
        phase = jnp.where(
            b < 2,
            jnp.where(b == 0, last_phase[0], last_phase[1]),
            jnp.where(b == 2, last_phase[2], last_phase[3]),
        )
        return phase == p

    @pl.loop(0, 4)
    def _(p):
        b = at_phase(p)

        @pl.when(jnp.logical_and(p == 0, native))
        def _():
            keep().wait()

        @pl.when(jnp.logical_and(p == 0, jnp.logical_not(native)))
        def _():
            whole().wait_recv()

        for k, slot in ((1, 1), (2, 2), (3, 0)):
            @pl.when(p == k)
            def _():
                source = at_phase(k)
                mine = part(g.at[source], d)
                remote(mine, mine, s1.at[0], hr.at[slot], c, d).wait_recv()
                pass_on(slot, source, d).start()
                if k == 1:
                    @pl.when(native)
                    def _():
                        for e in range(2):
                            send(far, e, s1, 0).start()
                pass_on(slot, source, 1 - d).wait_recv()

        project(b)
        for t in range(block // TILE):
            attend(b, b, TILE * t, TILE * t, TILE, True)

        @pl.loop(0, p)
        def _(r):
            other = at_phase(r)
            qb = jnp.maximum(b, other)
            kb = jnp.minimum(b, other)

            attend(qb, kb, 0, 0, block, False)

            @pl.when(jnp.logical_and(qb == other, complete(qb, p)))
            def _():
                finish(qb)

        @pl.when(complete(b, p))
        def _():
            finish(b)

    for b in range(4):
        own = jnp.logical_and(b == c, native)

        @pl.when(own)
        def _():
            home_own().wait()

        @pl.when(jnp.logical_not(own))
        def _():
            home(b).wait_send()

        rows = pl.ds(b * block, block)
        pltpu.make_async_copy(qkv.at[rows], qkv_out.at[rows], outs.at[0, b]).wait()
        pltpu.make_async_copy(act.at[rows], act_out.at[rows], outs.at[1, b]).wait()
        pltpu.make_async_copy(o.at[rows], o_out.at[rows], outs.at[2, b]).wait()

    @pl.when(native)
    def _():
        whole().wait_send()
        for e in range(2):
            send(far, e, s1, 0).wait_send()

    @pl.when(jnp.logical_not(native))
    def _():
        for e in range(2):
            send(side, e, s1, 1).wait_send()
            send(over, e, s2, 2).wait_send()

    for slot, source in ((1, side), (2, over), (0, far)):
        pass_on(slot, source, d).wait_send()
    for h in range(4):
        own = jnp.logical_and(h == pair, native)

        @pl.when(jnp.logical_not(own))
        def _():
            remote(att_ref.at[h], att_ref.at[h], hsems.at[h], hrecv.at[h], c, d).wait_recv()


def forward_pass(x, gain, w):
    count, width = x.shape
    length = 4 * count
    dma = pltpu.SemaphoreType.DMA
    return pl.pallas_call(
        forward_kernel,
        out_shape=(
            jax.ShapeDtypeStruct((4, count, 128), BF),
            jax.ShapeDtypeStruct((length, 384), BF),
            jax.ShapeDtypeStruct((length, 128), BF),
            jax.ShapeDtypeStruct((length, width), BF),
            jax.ShapeDtypeStruct((2, length), F32),
        ),
        in_specs=[VMEM] * 3,
        out_specs=(VMEM, ANY, ANY, ANY, VMEM),
        scratch_shapes=[
            pltpu.VMEM((4, count, width), BF),
            pltpu.VMEM((width, 384), BF),
            pltpu.VMEM((length, 384), BF),
            pltpu.VMEM((2, length, 128), BF),
            pltpu.VMEM((2, 80, length), BF),
            pltpu.VMEM((2, 80, length), F32),
            pltpu.VMEM((2, length), F32),
            pltpu.VMEM((length, 128), BF),
            pltpu.VMEM((length, width), BF),
            dma((2,)), dma, dma, dma((2,)), dma((2,)), dma((3,)), dma((3,)), dma((3,)),
            dma((4,)), dma((4,)), dma((3, 4)),
        ],
        compiler_params=params(collective_id=0, has_side_effects=True),
        name="forward_pass",
    )(x, gain, w)


def back_kernel(
    planes,
    datt_ref, qkv_ref, o_ref, lse_ref, act_hbm, x_hbm, gain_ref, w_hbm, dres_hbm, gp_ref, small_ref,
    tg_hbm, final_hbm, op_ref, os_ref, gg_ref,
    act_ref, x_ref, w_ref, dres_ref, do, qh, dh, kh, dq, dkv, delta, dsend, dhome, gq, dall,
    wire0, got0, wire1, got1, all2, sum1, back1, slots,
    wire3, got3, sum3, got4, back4, final,
    local, dsems, drecv, hsems, hrecv,
    send0, send1, send2, recv0, recv1, recv2, ret0, ret1, ssend, srecv,
    bsend, brecv, csend, crecv, cback, fsend, frecv, gsend, grecv, loads, stores,
):
    z = lax.axis_index("experts")
    c, d = coords()
    seq = sequence_of(c)
    column = lax.rem(c, 2)
    pair = 2 * (c // 2) + d
    side = 2 * (c // 2) + 1 - column
    over = 2 * (1 - c // 2) + column
    far = 3 - c
    native = d == seq
    length = qkv_ref.shape[0]
    block = length // 4
    width = gain_ref.shape[1]
    tq = tk = TILE
    tiles = length // TILE
    per = block // TILE
    counts = (2, 4, planes)
    places = (d, c, z)
    axes = ("dp", "context", "experts")

    def mate(stage, k):
        return {axes[stage]: lax.rem(places[stage] + k, counts[stage])}

    barrier = pltpu.get_barrier_semaphore()
    for k in range(1, 8):
        other = lax.rem(2 * c + d + k, 8)
        pl.semaphore_signal(
            barrier, inc=1, device_id={"context": other // 2, "dp": lax.rem(other, 2)},
            device_id_type=MESH,
        )
    for k in range(1, planes):
        pl.semaphore_signal(barrier, inc=1, device_id=mate(2, k), device_id_type=MESH)
    pl.semaphore_wait(barrier, 6 + planes)

    def copy(src, dst, send, recv, stage, k):
        return pltpu.make_async_remote_copy(
            src_ref=src, dst_ref=dst, send_sem=send, recv_sem=recv,
            device_id=mate(stage, k), device_id_type=MESH,
        )

    def scatter(h, go):
        chip = chip_of(d, h // 2)
        e = h % 2
        own = jnp.logical_and(chip == c, e == d)

        @pl.when(jnp.logical_and(own, go))
        def _():
            pltpu.make_async_copy(datt_ref.at[h], do.at[c], local.at[0]).start()

        @pl.when(jnp.logical_not(own))
        def _():
            op = remote(datt_ref.at[h], do.at[c], dsems.at[h], drecv.at[c], chip, e)
            op.start() if go else op.wait_send()

    for h in range(4):
        scatter(h, True)

    late = [
        pltpu.make_async_copy(source, target, loads.at[k])
        for k, (source, target) in enumerate(
            ((act_hbm, act_ref), (x_hbm, x_ref), (w_hbm, w_ref), (dres_hbm, dres_ref))
        )
    ]
    for op in late:
        op.start()

    low = lax.broadcasted_iota(jnp.int32, (1, 128), 1) < 64
    low_rows = lax.broadcasted_iota(jnp.int32, (128, 1), 0) < 64
    head_sum = (
        lax.broadcasted_iota(jnp.int32, (8, 128), 1) // 64
        == lax.broadcasted_iota(jnp.int32, (8, 128), 0)
    ).astype(F32)

    @pl.loop(0, tiles)
    def _(t):
        rows = pl.ds(pl.multiple_of(t * TILE, TILE), TILE)
        q = qkv_ref[rows, 0:128]
        zero = jnp.zeros_like(q)
        qh[0, rows, :] = jnp.where(low, q, zero)
        qh[1, rows, :] = jnp.where(low, zero, q)
        kt = jnp.transpose(qkv_ref[rows, 128:256].astype(F32)).astype(BF)
        zt = jnp.zeros_like(kt)
        kh[0, :, rows] = jnp.where(low_rows, kt, zt)
        kh[1, :, rows] = jnp.where(low_rows, zt, kt)
        dq[:, rows] = jnp.zeros((128, TILE), F32)
        dkv[rows, :] = jnp.zeros((TILE, 256), F32)

    gq[...] = jnp.zeros_like(gq)

    width_half = width // 2
    eighth = width_half // 4

    def small_start(stage, value):
        slots[stage, places[stage]] = value
        own = slots.at[stage, places[stage]]
        for k in range(1, counts[stage]):
            copy(own, own, ssend.at[stage, k - 1], srecv.at[stage, k - 1], stage, k).start()

    def small_sum(stage):
        own = slots.at[stage, places[stage]]
        for k in range(1, counts[stage]):
            copy(own, own, ssend.at[stage, k - 1], srecv.at[stage, k - 1], stage, k).wait()
        value = slots[stage, 0]
        for k in range(1, counts[stage]):
            value = value + slots[stage, k]
        return value

    def stage0():
        return copy(wire0, got0, send0, recv0, 0, 1)

    def stage1(k):
        rows = pl.ds(lax.rem(c + k, 4) * eighth, eighth)
        return copy(wire1.at[rows], got1.at[k - 1], send1.at[k - 1], recv1.at[k - 1], 1, k)

    def stage2(k):
        return copy(all2.at[z], all2.at[z], send2.at[k - 1], recv2.at[k - 1], 2, k)

    own1 = pl.ds(pl.multiple_of(c * eighth, eighth), eighth)

    def stage4(k):
        return copy(back1.at[d, own1], back1.at[d, own1], send1.at[k - 1], ret1.at[k - 1], 1, k)

    def stage5():
        return copy(back1.at[d], back1.at[d], send0, ret0, 0, 1)

    def early(t):
        @pl.when(t == 0)
        def _():
            wire0[...] = gp_ref[pl.ds(pl.multiple_of((1 - d) * width_half, width_half), width_half), :].astype(BF)
            stage0().start()
            small_start(0, small_ref[...])

        @pl.when(t == 1)
        def _():
            stage0().wait()
            mine = gp_ref[pl.ds(pl.multiple_of(d * width_half, width_half), width_half), :] + got0[...].astype(F32)
            sum1[...] = mine
            wire1[...] = mine.astype(BF)
            for k in (2, 1, 3):
                stage1(k).start()
            small_start(1, small_sum(0))

        @pl.when(t == 2)
        def _():
            for k in range(1, 4):
                stage1(k).wait()
            mine = sum1[own1, :]
            for k in range(3):
                mine = mine + got1[k].astype(F32)
            all2[z] = mine.astype(BF)
            for k in range(1, planes):
                stage2(k).start()
            small_start(2, small_sum(1))

        @pl.when(t == 3)
        def _():
            for k in range(1, planes):
                stage2(k).wait()
            mine = all2[0].astype(F32)
            for k in range(1, planes):
                mine = mine + all2[k].astype(F32)
            back1[d, own1, :] = mine.astype(BF)
            for k in (2, 1, 3):
                stage4(k).start()
            os_ref[...] = small_sum(2)

        @pl.when(t == 4)
        def _():
            for k in range(1, 4):
                stage4(k).wait()
            stage5().start()

        @pl.when(t == 5)
        def _():
            stage5().wait()
            for i in range(2):
                op_ref[i * width_half : (i + 1) * width_half, :] = back1[i].astype(F32)

    for source in (c, side, over, far):
        if source is c:
            @pl.when(native)
            def _():
                pltpu.make_async_copy(datt_ref.at[0], do.at[c], local.at[0]).wait()

            @pl.when(jnp.logical_not(native))
            def _():
                remote(do.at[c], do.at[c], dsems.at[0], drecv.at[c], c, d).wait_recv()
        else:
            remote(do.at[source], do.at[source], dsems.at[0], drecv.at[source], c, d).wait_recv()

        @pl.loop(0, per)
        def _(t):
            part = pl.ds(pl.multiple_of(t * TILE, TILE), TILE)
            rows = pl.ds(pl.multiple_of(source * block + t * TILE, TILE), TILE)
            g = do[source, part, :]
            zero = jnp.zeros_like(g)
            dh[0, rows, :] = jnp.where(low, g, zero)
            dh[1, rows, :] = jnp.where(low, zero, g)
            product = g.astype(F32) * o_ref[rows, :].astype(F32)
            delta[:, rows] = dotf(
                head_sum, product, ((1,), (1,)), precision=lax.Precision.HIGHEST
            )

    def step(i, j, masked):
        qrows = pl.ds(pl.multiple_of(i * tq, tq), tq)
        krows = pl.ds(pl.multiple_of(j * tk, tk), tk)
        k = qkv_ref[krows, 128:256]
        v = qkv_ref[krows, 256:384]
        dk = dv = dqt = 0.0
        for h in range(2):
            s = dotf(k, qh[h, qrows, :], ((1,), (1,)))
            p = jnp.exp(s - lse_ref[h : h + 1, qrows])
            if masked:
                kpos = lax.broadcasted_iota(jnp.int32, (tk, tq), 0)
                qpos = lax.broadcasted_iota(jnp.int32, (tk, tq), 1)
                p = jnp.where(kpos <= qpos, p, 0.0)
            dp = dotf(v, dh[h, qrows, :], ((1,), (1,)))
            ds = (p * (dp - delta[h : h + 1, qrows])).astype(BF)
            dv = dv + dotf(p.astype(BF), dh[h, qrows, :])
            dk = dk + dotf(ds, qh[h, qrows, :])
            dqt = dqt + dotf(kh[h, :, krows], ds)
        dq[:, qrows] = dq[:, qrows] + dqt
        dkv[krows, 0:128] = dkv[krows, 0:128] + dk
        dkv[krows, 128:256] = dkv[krows, 128:256] + dv

    for op in late:
        op.wait()

    def send_home(b, go):
        own = jnp.logical_and(b == c, native)

        @pl.when(own)
        def _():
            op = pltpu.make_async_copy(dsend.at[b], dhome.at[pair], local.at[1])
            op.start() if go else op.wait()

        @pl.when(jnp.logical_not(own))
        def _():
            op = remote(dsend.at[b], dhome.at[pair], hsems.at[b], hrecv.at[pair], b, seq)
            op.start() if go else op.wait_send()

    @pl.loop(0, tiles)
    def _(t):
        early(t)
        diagonal = jnp.where(d == 0, t, tiles - 1 - t)
        step(diagonal, diagonal, True)

        @pl.loop(1, tiles - t)
        def _(u):
            step(
                jnp.where(d == 0, t + u, tiles - 1 - t),
                jnp.where(d == 0, t, tiles - 1 - t - u),
                False,
            )

        @pl.when(lax.rem(t, per) == per - 1)
        def _():
            b = diagonal // per
            for half in range(per):
                rows = pl.ds(pl.multiple_of(b * block + half * TILE, TILE), TILE)
                part = slice(half * TILE, half * TILE + TILE)
                dsend[b, part, 0:128] = (jnp.transpose(dq[:, rows]) * 0.125).astype(BF)
                dsend[b, part, 128:384] = dkv[rows, :].astype(BF)
            for k in range(4):
                @pl.when(b == k)
                def _():
                    send_home(k, True)
            rows = pl.ds(pl.multiple_of(b * block, block), block)
            gq[...] = gq[...] + dotf(act_ref[rows, :], dsend[b], ((0,), (0,)))

    rest = gq.shape[0] // 2
    bit = rest // planes

    def next0():
        return remote(wire3, got3, bsend, brecv, side, d)

    def next1(k):
        rows = pl.ds(lax.rem(z + k, planes) * bit, bit)
        return copy(wire3.at[rows], got4.at[k - 1], csend.at[k - 1], crecv.at[k - 1], 2, k)

    own3 = pl.ds(pl.multiple_of(z * bit, bit), bit)

    def next2(k):
        return copy(back4.at[own3], back4.at[own3], csend.at[k - 1], cback.at[k - 1], 2, k)

    def next3(k):
        return copy(final.at[c, d], final.at[c, d], fsend.at[k - 1], frecv.at[k - 1], 1, k)

    def next4(k):
        chip = lax.rem(c + k, 4)
        return copy(final.at[chip, d], final.at[chip, d], gsend.at[k], grecv.at[chip], 0, 1)

    wire3[...] = gq[pl.ds(pl.multiple_of((1 - column) * rest, rest), rest), :].astype(BF)
    next0().start()
    for h in range(4):
        scatter(h, False)
    next0().wait()
    mine = gq[pl.ds(pl.multiple_of(column * rest, rest), rest), :] + got3[...].astype(F32)
    sum3[...] = mine
    wire3[...] = mine.astype(BF)
    for k in range(1, planes):
        next1(k).start()
    for k in range(1, planes):
        next1(k).wait()
    mine = sum3[own3, :]
    for k in range(planes - 1):
        mine = mine + got4[k].astype(F32)
    back4[own3, :] = mine.astype(BF)
    for k in range(1, planes):
        next2(k).start()

    for b in range(4):
        send_home(b, False)
    for h in range(4):
        own = jnp.logical_and(h == pair, native)

        @pl.when(jnp.logical_not(own))
        def _():
            remote(dhome.at[h], dhome.at[h], hsems.at[h], hrecv.at[h], c, d).wait_recv()

        for i in range(3):
            first = i * width + 128 * h
            dall[:, first : first + 128] = dhome[h, :, 128 * i : 128 * i + 128]

    def input_rows(first, last):
        @pl.loop(first, last)
        def _(t):
            rows = pl.ds(pl.multiple_of(t * 256, 256), 256)
            x = x_ref[rows, :].astype(F32)
            inv = lax.rsqrt(jnp.mean(x * x, axis=1, keepdims=True) + NORM_EPS)
            normed = x * inv
            scaled = dotf(dall[rows, :], w_ref[...], ((1,), (1,))) * gain_ref[...]
            inner = jnp.mean(scaled * normed, axis=1, keepdims=True)
            dres_ref[rows, :] = dres_ref[rows, :] + inv * (scaled - normed * inner)

    count = x_ref.shape[0] // 256
    input_rows(0, count // 2)
    for k in range(1, planes):
        next2(k).wait()
    final[c, d] = back4[...]
    for k in (2, 1, 3):
        next3(k).start()
    next4(0).start()
    input_rows(count // 2, count)
    result = pltpu.make_async_copy(dres_ref, tg_hbm, loads.at[0])
    result.start()
    for k in range(1, 4):
        next3(k).wait_send()
    for k in (1, 3, 2):
        chip = lax.rem(c + 4 - k, 4)
        copy(final.at[chip, d], final.at[chip, d], fsend.at[k - 1], frecv.at[k - 1], 1, k).wait_recv()
        next4(4 - k).start()
    for k in range(4):
        next4(k).wait_send()
    for chip in range(4):
        copy(final.at[chip, 1 - d], final.at[chip, 1 - d], gsend.at[chip], grecv.at[chip], 0, 1).wait_recv()
    spread = []
    for chip in range(4):
        for e in range(2):
            for i in range(3):
                rows = pl.ds((chip % 2) * rest, rest)
                cols = pl.ds(i * width + (2 * (chip // 2) + e) * 128, 128)
                op = pltpu.make_async_copy(
                    final.at[chip, e, :, pl.ds(128 * i, 128)],
                    final_hbm.at[rows, cols],
                    stores.at[len(spread)],
                )
                op.start()
                spread.append(op)
    for part in range(2):
        rows = slice(part * rest, (part + 1) * rest)
        weighted = 0.0
        for row in range(2):
            for e in range(2):
                for i in range(3):
                    first = i * width + (2 * row + e) * 128
                    weighted = weighted + w_ref[rows, first : first + 128].astype(F32) * final[
                        2 * row + part, e, :, 128 * i : 128 * i + 128
                    ].astype(F32)
        gg_ref[:, rows] = (
            dotf(jnp.ones((8, 128), F32), weighted, ((1,), (1,)), precision=lax.Precision.HIGHEST)
            / gain_ref[:, rows]
        )
    result.wait()
    for op in spread:
        op.wait()


def back_pass(d_att, qkv, o, lse, act, x, gain, w, d_res, g_proj, small, planes):
    length = qkv.shape[0]
    count, width = x.shape
    half = width // 2
    eighth = half // 4
    rest = width // 2
    most = max(4, planes)
    dma = pltpu.SemaphoreType.DMA
    return pl.pallas_call(
        functools.partial(back_kernel, planes),
        out_shape=(
            jax.ShapeDtypeStruct((count, width), F32),
            jax.ShapeDtypeStruct((width, 3 * width), BF),
            jax.ShapeDtypeStruct((width, width), F32),
            jax.ShapeDtypeStruct(small.shape, F32),
            jax.ShapeDtypeStruct((8, width), F32),
        ),
        in_specs=[VMEM, VMEM, VMEM, VMEM, ANY, ANY, VMEM, ANY, ANY, VMEM, VMEM],
        out_specs=(ANY, ANY, VMEM, VMEM, VMEM),
        scratch_shapes=[
            pltpu.VMEM(act.shape, BF),
            pltpu.VMEM(x.shape, BF),
            pltpu.VMEM(w.shape, BF),
            pltpu.VMEM(x.shape, F32),
            pltpu.VMEM((4, count, 128), BF),
            pltpu.VMEM((2, length, 128), BF),
            pltpu.VMEM((2, length, 128), BF),
            pltpu.VMEM((2, 128, length), BF),
            pltpu.VMEM((128, length), F32),
            pltpu.VMEM((length, 256), F32),
            pltpu.VMEM((8, length), F32),
            pltpu.VMEM((4, count, 384), BF),
            pltpu.VMEM((4, count, 384), BF),
            pltpu.VMEM((width, 384), F32),
            pltpu.VMEM((count, 3 * width), BF),
            pltpu.VMEM((half, width), BF),
            pltpu.VMEM((half, width), BF),
            pltpu.VMEM((half, width), BF),
            pltpu.VMEM((3, eighth, width), BF),
            pltpu.VMEM((planes, eighth, width), BF),
            pltpu.VMEM((half, width), F32),
            pltpu.VMEM((2, half, width), BF),
            pltpu.VMEM((3, most) + small.shape, F32),
            pltpu.VMEM((rest, 384), BF),
            pltpu.VMEM((rest, 384), BF),
            pltpu.VMEM((rest, 384), F32),
            pltpu.VMEM((planes - 1, rest // planes, 384), BF),
            pltpu.VMEM((rest, 384), BF),
            pltpu.VMEM((4, 2, rest, 384), BF),
            dma((2,)), dma((4,)), dma((4,)), dma((4,)), dma((4,)),
            dma, dma((3,)), dma((planes - 1,)),
            dma, dma((3,)), dma((planes - 1,)),
            dma, dma((3,)),
            dma((3, most - 1)), dma((3, most - 1)),
            dma, dma, dma((planes - 1,)), dma((planes - 1,)), dma((planes - 1,)),
            dma((3,)), dma((3,)), dma((4,)), dma((4,)), dma((4,)), dma((24,)),
        ],
        compiler_params=params(collective_id=2, has_side_effects=True),
        name="back_pass",
    )(d_att, qkv, o, lse, act, x, gain, w, d_res, g_proj, small)


def mix_kernel(
    stride, capacity, local, choices,
    x_ref, att_ref, wo_ref, gain_ref, router_ref, slot_ref, pair_ref, gout_ref,
    res_ref, mix_ref, wts_ref, place_ref, send_ref,
    att,
):
    tokens = x_ref.shape[0]
    pairs = pair_ref.shape[1]
    experts = router_ref.shape[1]
    members = tokens * choices // pairs
    for h in range(4):
        att[:, 128 * h : 128 * h + 128] = att_ref[h]

    @pl.loop(0, tokens // 256)
    def _(t):
        rows = pl.ds(pl.multiple_of(t * 256, 256), 256)
        res = x_ref[rows, :].astype(F32) + dotf(att[rows, :], wo_ref[...])
        inv = lax.rsqrt(jnp.mean(res * res, axis=1, keepdims=True) + NORM_EPS)
        res_ref[rows, :] = res
        mix_ref[rows, :] = (res * inv * gain_ref[...]).astype(BF)

    routes = pair_ref[0:1, :]
    order = pair_ref[1:2, :]
    eye = lax.broadcasted_iota(jnp.int32, (pairs, pairs), 0) == lax.broadcasted_iota(
        jnp.int32, (pairs, pairs), 1
    )
    zero = jnp.zeros((pairs, pairs), F32)

    def as_column(row):
        return jnp.sum(jnp.where(eye, row.astype(F32), zero), axis=1, keepdims=True)

    route_col = as_column(routes)
    order_col = as_column(order)
    ahead = jnp.logical_and(route_col == routes.astype(F32), order_col < order.astype(F32))
    rank = jnp.sum(ahead.astype(F32), axis=0, keepdims=True).astype(jnp.int32)
    slots = place_ref.shape[0]
    block = lax.div(routes, local)
    place = block * stride + (routes - block * local) * capacity + rank
    place = jnp.where(rank < capacity, place, slots)
    spread = (lax.broadcasted_iota(jnp.int32, (slots, pairs), 0) == place).astype(BF)
    place_ref[...] = spread

    pick = (lax.broadcasted_iota(jnp.int32, (experts, pairs), 0) == routes).astype(F32)
    columns = dotf(router_ref[...].astype(F32), pick).astype(BF)
    chosen = dotf(columns, mix_ref[...], ((0,), (1,)))
    group = lax.broadcasted_iota(jnp.int32, (pairs, 1), 0) // choices
    member = group == slot_ref[...] // members
    chosen = jnp.where(member, chosen, MASKED)
    peak = jnp.max(chosen, axis=1, keepdims=True)
    weight = jnp.where(member, jnp.exp(chosen - peak), 0.0)
    weight = weight / jnp.sum(weight, axis=1, keepdims=True)
    wts_ref[...] = weight
    low = weight.astype(BF)
    width = mix_ref.shape[1]
    mixed = dotf(low, mix_ref[...]).astype(BF)
    send_ref[:, 0:width] = dotf(spread, mixed).astype(BF)
    dy = dotf(low, gout_ref[...]).astype(BF)
    send_ref[:, width:] = dotf(spread, dy).astype(BF)


def gelu_parts(x):
    scale = np.float32(np.sqrt(2.0 / np.pi))
    square = x * x
    t = jnp.tanh(scale * (x + np.float32(0.044715) * (square * x)))
    half = 0.5 * (1.0 + t)
    slope = half + (0.5 * x) * (1.0 - t * t) * (
        scale * (1.0 + np.float32(3 * 0.044715) * square)
    )
    return x * half, slope


def expert_kernel(steps, recv_ref, pick_ref, win_ref, wout_ref, rows_ref, ret_ref, y, dx):
    e = pl.program_id(0)
    f = pl.program_id(1)
    width = win_ref.shape[1]

    @pl.when(f == 0)
    def _():
        rows_ref[0] = dotf(pick_ref[0], recv_ref[...]).astype(BF)
        y[...] = jnp.zeros_like(y)
        dx[...] = jnp.zeros_like(dx)

    @pl.when(jnp.logical_and(e == 0, f == 0))
    def _():
        ret_ref[...] = jnp.zeros_like(ret_ref)

    x = rows_ref[0, :, 0:width]
    dy = rows_ref[0, :, width:]
    hidden, slope = gelu_parts(dotf(x, win_ref[0]))
    y[...] += dotf(hidden.astype(BF), wout_ref[0])
    d_pre = (dotf(dy, wout_ref[0], ((1,), (1,))) * slope).astype(BF)
    dx[...] += dotf(d_pre, win_ref[0], ((1,), (1,)))

    @pl.when(f == steps - 1)
    def _():
        both = jnp.concatenate([y[...].astype(BF), dx[...].astype(BF)], axis=1)
        ret_ref[...] += dotf(pick_ref[0], both, ((0,), (0,))).astype(BF)


def expert_rows(recv, pick, w_in, w_out):
    local, count, total = pick.shape
    _, width, hidden = w_in.shape
    chunk = 512
    steps = hidden // chunk
    return pl.pallas_call(
        functools.partial(expert_kernel, steps),
        grid=(local, steps),
        out_shape=(
            jax.ShapeDtypeStruct((local, count, 2 * width), BF),
            jax.ShapeDtypeStruct((total, 2 * width), BF),
        ),
        in_specs=[
            pl.BlockSpec((total, 2 * width), lambda e, f: (0, 0)),
            pl.BlockSpec((1, count, total), lambda e, f: (e, 0, 0)),
            pl.BlockSpec((1, width, chunk), lambda e, f: (e, 0, f)),
            pl.BlockSpec((1, chunk, width), lambda e, f: (e, f, 0)),
        ],
        out_specs=(
            pl.BlockSpec((1, count, 2 * width), lambda e, f: (e, 0, 0)),
            pl.BlockSpec((total, 2 * width), lambda e, f: (0, 0)),
        ),
        scratch_shapes=[pltpu.VMEM((count, width), F32), pltpu.VMEM((count, width), F32)],
        compiler_params=params(),
        name="expert_rows",
    )(recv, pick, w_in, w_out)


def expert_grad_kernel(rows_ref, win_ref, wout_ref, gin_ref, gout_ref, xt, dy, dyt):
    width = win_ref.shape[1]
    copies, _, count, _ = rows_ref.shape

    @pl.when(pl.program_id(1) == 0)
    def _():
        x = jnp.concatenate([rows_ref[k, 0, :, 0:width] for k in range(copies)], axis=0)
        xt[...] = jnp.transpose(x.astype(F32)).astype(BF)
        value = jnp.concatenate([rows_ref[k, 0, :, width:] for k in range(copies)], axis=0)
        dy[...] = value
        dyt[...] = jnp.transpose(value.astype(F32)).astype(BF)

    chunk = wout_ref.shape[1]
    parts = [slice(0, chunk // 2), slice(chunk // 2, chunk)]
    first = []
    for part in parts:
        win_t = jnp.transpose(win_ref[0, :, part].astype(F32)).astype(BF)
        first.append((dotf(win_t, xt[...]), dotf(wout_ref[0, part, :], dyt[...])))
    second = []
    for pre, d_hidden in first:
        hidden, slope = gelu_parts(pre)
        second.append((hidden.astype(BF), (d_hidden * slope).astype(BF)))
    for part, (hidden, d_pre) in zip(parts, second):
        gin_ref[0, :, part] = dotf(xt[...], d_pre, ((1,), (1,)))
        gout_ref[0, part, :] = dotf(hidden, dy[...])


def expert_grads(rows, w_in, w_out):
    copies, local, count, double = rows.shape
    _, width, hidden = w_in.shape
    chunk = 512
    return pl.pallas_call(
        expert_grad_kernel,
        grid=(local, hidden // chunk),
        out_shape=(
            jax.ShapeDtypeStruct(w_in.shape, F32),
            jax.ShapeDtypeStruct(w_out.shape, F32),
        ),
        in_specs=[
            pl.BlockSpec((copies, 1, count, double), lambda e, f: (0, e, 0, 0)),
            pl.BlockSpec((1, width, chunk), lambda e, f: (e, 0, f)),
            pl.BlockSpec((1, chunk, width), lambda e, f: (e, f, 0)),
        ],
        out_specs=(
            pl.BlockSpec((1, width, chunk), lambda e, f: (e, 0, f)),
            pl.BlockSpec((1, chunk, width), lambda e, f: (e, f, 0)),
        ),
        scratch_shapes=[
            pltpu.VMEM((width, copies * count), BF),
            pltpu.VMEM((copies * count, width), BF),
            pltpu.VMEM((width, copies * count), BF),
        ],
        compiler_params=params(),
        cost_estimate=pl.CostEstimate(
            flops=8 * copies * local * count * width * hidden,
            bytes_accessed=12 * local * width * hidden,
            transcendentals=copies * local * count * hidden,
        ),
        name="expert_grads",
    )(rows, w_in, w_out)


def unmix_kernel(
    choices,
    res_ref, mix_ref, wts_ref, place_ref, ret_ref, gout_ref, att_ref, wo_ref, gain_ref, router_ref,
    pair_ref,
    out_ref, dres_ref, datt_ref, gproj_ref, small_ref,
    att, dproj, back,
):
    tokens, width = res_ref.shape
    experts = router_ref.shape[1]
    pairs = pair_ref.shape[1]
    rows_back = dotf(place_ref[...], ret_ref[...], ((0,), (0,))).astype(BF)
    y = rows_back[:, 0:width]
    dm = rows_back[:, width:]
    weight = wts_ref[...]
    low = weight.astype(BF)
    dw = dotf(y, gout_ref[...], ((1,), (1,))) + dotf(dm, mix_ref[...], ((1,), (1,)))
    d_chosen = weight * (dw - jnp.sum(weight * dw, axis=1, keepdims=True))
    pick = (
        lax.broadcasted_iota(jnp.int32, (experts, pairs), 0) == pair_ref[0:1, :]
    ).astype(BF)
    d_logits = dotf(pick, d_chosen.astype(BF)).astype(BF)
    small_ref[0:experts, :] = dotf(d_logits, mix_ref[...])
    small_ref[experts:, :] = jnp.zeros((small_ref.shape[0] - experts, width), F32)
    spare = back.shape[0] - pairs - experts
    back[0:pairs, :] = low
    back[pairs : pairs + experts, :] = d_logits
    if spare:
        back[pairs + experts :, :] = jnp.zeros((spare, tokens), BF)
    router_t = jnp.transpose(
        jnp.concatenate(
            [router_ref[...].astype(F32), jnp.zeros((width, 128 - experts), F32)], axis=1
        )
    ).astype(BF)[0 : back.shape[0] - pairs, :]
    for h in range(4):
        att[:, 128 * h : 128 * h + 128] = att_ref[h]
    rhs = jnp.concatenate([dm, router_t], axis=0)
    gain_grad = jnp.zeros((1, width), F32)
    for t in range(tokens // 256):
        rows = slice(t * 256, t * 256 + 256)
        res = res_ref[rows, :]
        combined = dotf(low[:, rows], y, ((0,), (0,)))
        out_ref[rows, :] = (res + combined).astype(BF)
        d_mix = dotf(back[:, rows], rhs, ((0,), (0,)))
        inv = lax.rsqrt(jnp.mean(res * res, axis=1, keepdims=True) + NORM_EPS)
        normed = res * inv
        scaled = d_mix * gain_ref[...]
        gain_grad = gain_grad + jnp.sum(d_mix * normed, axis=0, keepdims=True)
        inner = jnp.mean(scaled * normed, axis=1, keepdims=True)
        d_res = gout_ref[rows, :].astype(F32) + inv * (scaled - normed * inner)
        dres_ref[rows, :] = d_res
        d_low = d_res.astype(BF)
        dproj[rows, :] = d_low
        d_att = dotf(d_low, wo_ref[...], ((1,), (1,))).astype(BF)
        for h in range(4):
            datt_ref[h, rows, :] = d_att[:, 128 * h : 128 * h + 128]
    small_ref[experts : experts + 1, :] = gain_grad
    gproj_ref[...] = dotf(att[...], dproj[...], ((0,), (0,)))


def pick_rows(sources, local, capacity, stride):
    pick = np.zeros((local, sources * capacity, sources * stride), np.float32)
    for e in range(local):
        for r in range(sources * capacity):
            pick[e, r, (r // capacity) * stride + e * capacity + r % capacity] = 1.0
    return pick


def per_device(
    planes,
    tokens,
    attn_gain,
    mix_gain,
    query_key_value_weight,
    output_weight,
    router_weight,
    w_in,
    w_exp_out,
    out_grad,
    group_slot,
    group_routes,
    route_order,
):
    x = tokens[0]
    gout = out_grad[0]
    count, width = x.shape
    groups, choices = group_routes.shape
    pairs = groups * choices
    experts = router_weight.shape[1]
    local = w_in.shape[0]
    sources = experts // local
    capacity = 5 * groups * choices // (4 * experts)
    stride = -(-local * capacity // 16) * 16
    slots = sources * stride
    small_rows = -(-(experts + 2) // 8) * 8
    gain_one = attn_gain.reshape(1, width)
    gain_two = mix_gain.reshape(1, width)
    pair_table = jnp.stack([group_routes.reshape(-1), route_order.reshape(-1)])

    att, qkv, o, act, lse = forward_pass(x, gain_one, query_key_value_weight)

    res, mix, weights, place, send = pl.pallas_call(
        functools.partial(mix_kernel, stride, capacity, local, choices),
        out_shape=(
            jax.ShapeDtypeStruct((count, width), F32),
            jax.ShapeDtypeStruct((count, width), BF),
            jax.ShapeDtypeStruct((pairs, count), F32),
            jax.ShapeDtypeStruct((slots, pairs), BF),
            jax.ShapeDtypeStruct((slots, 2 * width), BF),
        ),
        in_specs=[VMEM] * 8,
        out_specs=(VMEM,) * 5,
        scratch_shapes=[pltpu.VMEM((count, width), BF)],
        compiler_params=params(),
        name="mix",
    )(x, att, output_weight, gain_two, router_weight, group_slot, pair_table, gout)

    recv = lax.all_to_all(
        send.reshape(sources, stride, 2 * width), "experts", split_axis=0, concat_axis=0, tiled=True
    ).reshape(slots, 2 * width)
    pick = jnp.asarray(pick_rows(sources, local, capacity, stride), BF)
    rows, ret = expert_rows(recv, pick, w_in, w_exp_out)
    ret = lax.all_to_all(
        ret.reshape(sources, stride, 2 * width), "experts", split_axis=0, concat_axis=0, tiled=True
    ).reshape(slots, 2 * width)
    all_rows = lax.all_gather(rows, ("context", "dp"), axis=0)

    layer_out, d_res, d_att, g_proj, small = pl.pallas_call(
        functools.partial(unmix_kernel, choices),
        out_shape=(
            jax.ShapeDtypeStruct((count, width), BF),
            jax.ShapeDtypeStruct((count, width), F32),
            jax.ShapeDtypeStruct((4, count, 128), BF),
            jax.ShapeDtypeStruct((width, width), F32),
            jax.ShapeDtypeStruct((small_rows, width), F32),
        ),
        in_specs=[VMEM] * 11,
        out_specs=(VMEM,) * 5,
        scratch_shapes=[
            pltpu.VMEM((count, width), BF),
            pltpu.VMEM((count, width), BF),
            pltpu.VMEM((pairs + -(-experts // 16) * 16, count), BF),
        ],
        compiler_params=params(),
        name="unmix",
    )(
        res, mix, weights, place, ret, gout, att, output_weight, gain_two, router_weight, pair_table
    )

    token_grad, qkv_grad, proj_grad, small, g_one = back_pass(
        d_att, qkv, o, lse, act, x, gain_one, query_key_value_weight, d_res, g_proj, small, planes
    )
    g_in, g_out = expert_grads(all_rows, w_in, w_exp_out)
    return (
        layer_out[None],
        token_grad[None],
        g_one[0],
        small[experts],
        qkv_grad.astype(F32),
        proj_grad,
        jnp.transpose(small[:experts]),
        g_in,
        g_out,
    )


def solution(mesh):
    token_spec = P(("experts", "dp"), "context", None)
    pair_spec = P(("experts", "context", "dp"), None)
    expert_spec = P("experts", None, None)
    return jax.shard_map(
        functools.partial(per_device, mesh.shape["experts"]),
        mesh=mesh,
        in_specs=(
            token_spec, P(), P(), P(), P(), P(), expert_spec, expert_spec, token_spec,
            P(("experts", "dp"), "context"), pair_spec, pair_spec,
        ),
        out_specs=(
            token_spec, token_spec, P(), P(), P(), P(), P(), expert_spec, expert_spec,
        ),
        check_vma=False,
    )
```
